128 devices in a mesh: dom: 16 (over x, y_hi, core), phase: 2 (over y_lo), feat: 4 (over z).
Axes of the slice: x: 4, y: 4 (y_hi: 2, y_lo: 2; y = y_hi * 2 + y_lo), z: 4, core: 2. Of those that a mesh axis runs over, the one named last changes fastest.
Arguments:
- node_in: bfloat16 [524288, 256], P(('dom', 'phase', 'feat')), may hold values from -6 to 6
- out_cot: bfloat16 [524288, 256], P(('dom', 'phase', 'feat')), may hold values from -6 to 6
- adjacency: bfloat16 [4096, 4, 128, 128], P(('dom', 'phase', 'feat')), may hold values from -0.25 to 0.25
- tile_nbrs: int32 [4096, 4], P(('dom', 'phase', 'feat')), may hold values from 0 to 47, as said below
- bound_tiles: int32 [128, 2, 8], P(('dom', 'phase', 'feat')), may hold values from 0 to 15, as said below
- live_tiles: int32 [128], P(('dom', 'phase', 'feat')), may hold values from 16 to 32, as said below
- w_self: bfloat16 [2, 256, 256], replicated, may hold values from -0.25 to 0.25
- w_nbr: bfloat16 [2, 256, 256], replicated, may hold values from -0.25 to 0.25
- pre_bias: float32 [2, 256], replicated, may hold values from -3 to 3
- w_out: bfloat16 [2, 256, 256], replicated, may hold values from -0.375 to 0.375
Outputs:
- section_out: bfloat16 [2, 524288, 256], P(None, ('dom', 'phase', 'feat'))
- section_in_grad: bfloat16 [2, 524288, 256], P(None, ('dom', 'phase', 'feat'))
- grad_self: float32 [2, 256, 256], replicated
- grad_nbr: float32 [2, 256, 256], replicated
- grad_bias: float32 [2, 256], replicated
- grad_out: float32 [2, 256, 256], replicated
The draws below stay inside these ranges and needn't reach their ends.
Inputs may be any that keep to these rules, and one draw needn't show every extreme that they name: `live_tiles`: some partition has all 32 tiles live. `bound_tiles`: for each partition the 16 entries are the tiles 0 to 15, each once. `tile_nbrs`: slot 0 of local tile i is i; every entry of a live tile names a live own tile (below 32) or an extended tile (from 32 on); each extended tile is named by some live tile; all entries of a tile that is not live are i.
All inputs are finite; a program needn't handle non-finite values.
Results may differ from the reference program's by a relative error of at most 0.008.
Values may be sent and summed in bfloat16 or wider, within the bound.
A program may use at most 192 MiB of HBM per device.

```python
import jax
import jax.numpy as jnp
from jax import lax

HID = 256
TILE = 128
SLOTS = 4
TILES = 32
EDGE_TILES = 8
PARTS_SIZE = 128
NODE_TILES = 4096
NODES = 524288


def live_counts(key):
    counts = jax.random.randint(jax.random.fold_in(key, 11), (PARTS_SIZE,), TILES // 2, TILES + 1)
    full_part = jax.random.randint(jax.random.fold_in(key, 12), (), 0, PARTS_SIZE)
    small_part = jax.random.randint(jax.random.fold_in(key, 13), (), 0, PARTS_SIZE)
    positions = jnp.arange(PARTS_SIZE)
    counts = jnp.where(positions == small_part, TILES // 2, counts)
    counts = jnp.where(positions == full_part, TILES, counts)
    return counts.astype(jnp.int32)


def draw_live_tiles(key, part):
    return live_counts(key)


def draw_bound_tiles(key, part):
    half_tiles = TILES // 2
    scores = jax.random.randint(jax.random.fold_in(key, 21), (PARTS_SIZE, half_tiles), 0, 1 << 20) * half_tiles + jnp.arange(half_tiles)[None, :]
    ranked = jnp.argsort(scores, axis=1).astype(jnp.int32)
    return ranked.reshape(PARTS_SIZE, 2, EDGE_TILES)


def draw_tile_nbrs(key, part):
    counts = live_counts(key)
    raw_pick = jax.random.randint(jax.random.fold_in(key, 31), (PARTS_SIZE, TILES, SLOTS), 0, TILES + 2 * EDGE_TILES)
    local_pick = raw_pick % counts[:, None, None]
    chosen = jnp.where(raw_pick < TILES, local_pick, raw_pick)
    own_tile = jnp.broadcast_to(jnp.arange(TILES)[None, :, None], (PARTS_SIZE, TILES, SLOTS))
    slot_index = jnp.broadcast_to(jnp.arange(SLOTS)[None, None, :], (PARTS_SIZE, TILES, SLOTS))
    chosen = jnp.where(slot_index == 0, own_tile, chosen)
    chosen = jnp.where((slot_index == 1) & (own_tile < 2 * EDGE_TILES), TILES + own_tile, chosen)
    chosen = jnp.where(own_tile >= counts[:, None, None], own_tile, chosen)
    return chosen.reshape(PARTS_SIZE * TILES, SLOTS).astype(jnp.int32)


def steps_of(own_key, extent, shards, least, high):
    def one(dim, shards_of):
        steps = jax.random.uniform(jax.random.fold_in(jax.random.fold_in(own_key, 6), dim), (shards_of,), jnp.float32, least / len(shards), high / len(shards))
        return jnp.repeat(jnp.exp(steps), extent[dim] // shards_of).reshape((-1,) + (1,) * (len(extent) - dim - 1))

    gain = one(*shards[0])
    for cut in shards[1:]:
        gain = gain * one(*cut)
    return gain


def noise(own_key, shape, deviation, limit, split=(), held_as=jnp.bfloat16):
    values = jax.random.normal(own_key, shape, jnp.float32) * deviation
    if len(split) > 0:
        values = steps_of(own_key, shape, split, -0.22, 0.18) * values
    return jnp.clip(values, min=-limit, max=limit).astype(held_as)


def setup_inputs(seed: int = 0) -> dict:
    streams_of = jax.random.split(jax.random.key(seed), 11)
    return {
        "node_in": noise(streams_of[0], (NODES, HID), 1.0, 6.0, ((0, 128),)),
        "out_cot": noise(streams_of[1], (NODES, HID), 1.0, 6.0, ((0, 128),)),
        "adjacency": noise(streams_of[2], (NODE_TILES, SLOTS, TILE, TILE), (TILE * SLOTS) ** -0.5, 0.25, ((0, 128),)),
        "tile_nbrs": draw_tile_nbrs(jax.random.fold_in(streams_of[10], 71), 0),
        "bound_tiles": draw_bound_tiles(jax.random.fold_in(streams_of[10], 71), 0),
        "live_tiles": draw_live_tiles(jax.random.fold_in(streams_of[10], 71), 0),
        "w_self": noise(streams_of[6], (2, HID, HID), (2 * HID) ** -0.5, 0.25),
        "w_nbr": noise(streams_of[7], (2, HID, HID), (2 * HID) ** -0.5, 0.25),
        "pre_bias": noise(streams_of[8], (2, HID), 0.5, 3.0, (), jnp.float32),
        "w_out": noise(streams_of[9], (2, HID, HID), HID ** -0.5, 0.375),
    }


def silu_slope(pre_act):
    sigma = jax.nn.sigmoid(pre_act)
    return sigma * (1.0 + pre_act * (1.0 - sigma))


def tile_pick(node_tiles, index_rows):
    return jax.vmap(lambda block_rows, chosen: block_rows[chosen])(node_tiles, index_rows)


def extend_tiles(node_tiles, bound_tiles):
    west_send = tile_pick(node_tiles, bound_tiles[:, 0])
    east_send = tile_pick(node_tiles, bound_tiles[:, 1])
    return jnp.concatenate([node_tiles, jnp.roll(east_send, 1, axis=0), jnp.roll(west_send, -1, axis=0)], axis=1)


def aggregate(extended, neighbours, adj_tiles):
    def one_part(operands):
        ext_part, nbr_part, adj_part = operands
        picked = ext_part[nbr_part]
        return jnp.einsum("tkij,tkjc->tic", adj_part.astype(jnp.float32), picked.astype(jnp.float32))
    return lax.map(one_part, (extended, neighbours, adj_tiles))


def spread_back(delta_tiles, neighbours, adj_tiles, bound_tiles):
    def one_part(operands):
        delta_part, nbr_part, adj_part = operands
        contrib = jnp.einsum("tkij,tic->tkjc", adj_part.astype(jnp.float32), delta_part.astype(jnp.float32))
        return jax.ops.segment_sum(contrib.reshape(TILES * SLOTS, TILE, -1), nbr_part.reshape(-1), num_segments=TILES + 2 * EDGE_TILES)
    collected = lax.map(one_part, (delta_tiles, neighbours, adj_tiles))
    local_part = collected[:, :TILES]
    west_part = collected[:, TILES:TILES + EDGE_TILES]
    east_part = collected[:, TILES + EDGE_TILES:]
    add_rows = jax.vmap(lambda block_rows, chosen, values: block_rows.at[chosen].add(values))
    local_part = add_rows(local_part, bound_tiles[:, 1], jnp.roll(west_part, -1, axis=0))
    local_part = add_rows(local_part, bound_tiles[:, 0], jnp.roll(east_part, 1, axis=0))
    return local_part


def forward(features, w_self, w_nbr, pre_bias, w_out, neighbours, adj_tiles, bound_tiles, row_mask):
    node_tiles = features.reshape(PARTS_SIZE, TILES, TILE, HID)
    summed = aggregate(extend_tiles(node_tiles, bound_tiles), neighbours, adj_tiles)
    gathered = summed.reshape(NODES, HID).astype(jnp.bfloat16)
    pre_act = jnp.dot(features, w_self, preferred_element_type=jnp.float32) + jnp.dot(gathered, w_nbr, preferred_element_type=jnp.float32) + pre_bias
    hidden = jax.nn.silu(pre_act).astype(jnp.bfloat16)
    result = (row_mask * (features.astype(jnp.float32) + jnp.dot(hidden, w_out, preferred_element_type=jnp.float32))).astype(jnp.bfloat16)
    return result, (features, gathered, pre_act, hidden)


def backward(upstream, saved_state, w_self, w_nbr, w_out, neighbours, adj_tiles, bound_tiles, row_mask):
    features, gathered, pre_act, hidden = saved_state
    masked = (upstream.astype(jnp.float32) * row_mask).astype(jnp.bfloat16)
    grad_out = jnp.dot(hidden.T, masked, preferred_element_type=jnp.float32)
    grad_hidden = jnp.dot(masked, w_out.T, preferred_element_type=jnp.float32)
    grad_pre = (grad_hidden * silu_slope(pre_act)).astype(jnp.bfloat16)
    grad_self = jnp.dot(features.T, grad_pre, preferred_element_type=jnp.float32)
    grad_nbr = jnp.dot(gathered.T, grad_pre, preferred_element_type=jnp.float32)
    grad_bias = jnp.sum(grad_pre.astype(jnp.float32), axis=0)
    direct = masked.astype(jnp.float32) + jnp.dot(grad_pre, w_self.T, preferred_element_type=jnp.float32)
    grad_gathered = jnp.dot(grad_pre, w_nbr.T, preferred_element_type=jnp.float32).astype(jnp.bfloat16)
    returned = spread_back(grad_gathered.reshape(PARTS_SIZE, TILES, TILE, HID), neighbours, adj_tiles, bound_tiles)
    grad_in = (direct + returned.reshape(NODES, HID)).astype(jnp.bfloat16)
    return grad_in, (grad_self, grad_nbr, grad_bias, grad_out)


def reference(node_in, out_cot, adjacency, tile_nbrs, bound_tiles, live_tiles, w_self, w_nbr, pre_bias, w_out):
    tile_live = (jnp.arange(TILES)[None, :] < live_tiles[:, None]).astype(jnp.float32)
    row_mask = jnp.repeat(tile_live.reshape(-1), TILE)[:, None]
    neighbours = tile_nbrs.reshape(PARTS_SIZE, TILES, SLOTS)
    adj_tiles = adjacency.reshape(PARTS_SIZE, TILES, SLOTS, TILE, TILE)
    first_out, first_saved = forward(node_in, w_self[0], w_nbr[0], pre_bias[0], w_out[0], neighbours, adj_tiles, bound_tiles, row_mask)
    second_out, second_saved = forward(first_out, w_self[1], w_nbr[1], pre_bias[1], w_out[1], neighbours, adj_tiles, bound_tiles, row_mask)
    grad_mid, later_grads = backward(out_cot, second_saved, w_self[1], w_nbr[1], w_out[1], neighbours, adj_tiles, bound_tiles, row_mask)
    grad_first, early_grads = backward(grad_mid, first_saved, w_self[0], w_nbr[0], w_out[0], neighbours, adj_tiles, bound_tiles, row_mask)
    return (jnp.stack([first_out, second_out]), jnp.stack([grad_first, grad_mid]),
            jnp.stack([early_grads[0], later_grads[0]]), jnp.stack([early_grads[1], later_grads[1]]),
            jnp.stack([early_grads[2], later_grads[2]]), jnp.stack([early_grads[3], later_grads[3]]))
```

```python
import functools

import jax
import jax.numpy as jnp
from jax import lax
from jax.experimental import pallas as pl
from jax.experimental.pallas import tpu as pltpu
from jax.sharding import PartitionSpec as P

AXES = ("dom", "phase", "feat")
MESH = pl.DeviceIdType.MESH
BF = jnp.bfloat16
F32 = jnp.float32
NT = 32
LENT = 16
ROWS = 128
HID = 256
PAIRS = 96
GROUP = 48
GRADS = 1024


def dot(a, b):
    return lax.dot_general(a, b, (((1,), (0,)), ((), ())), preferred_element_type=F32)


def dot_rows(a, b):
    return lax.dot_general(a, b, (((0,), (0,)), ((), ())), preferred_element_type=F32)


def chip_id(x, y, core, z):
    return (x * 4 + (y // 2) * 2 + core, y % 2, z)


def part_id(part):
    return (part // 8, (part // 4) % 2, part % 4)


def build_tables(nbr_vec, bound_sm, tab_v):
    i32 = jnp.int32
    lane32 = lax.broadcasted_iota(i32, (NT, 128), 1)
    row32 = lax.broadcasted_iota(i32, (NT, 128), 0)
    spread = jnp.zeros((NT, 128), i32)
    for k in range(4):
        here = (lane32 // 4 == row32) & (lane32 % 4 == k)
        spread = spread + jnp.where(here, jnp.broadcast_to(nbr_vec[:, k : k + 1], (NT, 128)), 0)
    target = jnp.sum(spread, axis=0, keepdims=True)
    lane = lax.broadcasted_iota(i32, (1, 128), 1)
    key = jnp.where(lane % 4 == 0, 4096, jnp.where(lane // 4 < LENT, 256, 0) + target)
    li = lax.broadcasted_iota(i32, (128, 128), 1)
    ri = lax.broadcasted_iota(i32, (128, 128), 0)
    key_l = jnp.broadcast_to(key, (128, 128))
    key_c = jnp.sum(jnp.where(li == ri, key_l, 0), axis=1, keepdims=True)
    key_r = jnp.broadcast_to(key_c, (128, 128))
    before = (key_l < key_r) | ((key_l == key_r) & (li < ri))
    rank = jnp.sum(jnp.where(before, 1, 0), axis=1, keepdims=True)
    same = jnp.sum(jnp.where((key_l == key_r) & (li < ri), 1, 0), axis=1, keepdims=True)
    place = jnp.broadcast_to(rank, (128, 128)) == li
    order = jnp.sum(jnp.where(place, ri, 0), axis=0, keepdims=True)
    joins = jnp.sum(jnp.where(place, jnp.broadcast_to(same, (128, 128)), 0), axis=0, keepdims=True)
    slot = lane
    for q in range(LENT):
        slot = jnp.where(lane == bound_sm[0, q // 8, q % 8], q, slot)
    rows = [slot, order, joins]
    for base in (0, 256):
        upto = jnp.sum(jnp.where(key_r <= li + base, 1, 0), axis=0, keepdims=True) - 1
        rows.append(jnp.maximum(upto, 0))
        rows.append(jnp.sum(jnp.where(key_r == li + base, 1, 0), axis=0, keepdims=True))
    for n, row in enumerate(rows):
        tab_v[n : n + 1, :] = row


def mega(
    node_h, cot_h, adj_h, nbr_v, nbr_s, bound_s, live_s, wself_h, wnbr_h, bias_v, wout_h,
    out_h, grad_h, sums_h,
    adj, adj_t, cot, lent, ext0, ext1, agg0, agg1, act0, act1, slope0, dpre, dagg, scan, direct, mid,
    ret1, ret0, send1, send0, w_in, w_out, w_out_t, w_self_t, w_nbr_t,
    total, pack, rc, rx, ry, rz, full, tab_v, tab,
    load_sem, tab_sem, store_sem, hs, hr, gs, gr,
):
    dom, phase, feat = (lax.axis_index(a) for a in AXES)
    x, core = dom // 4, dom % 2
    y = ((dom // 2) % 2) * 2 + phase
    z = feat
    part = dom * 8 + phase * 4 + feat
    west = part_id((part + 127) % 128)
    east = part_id((part + 1) % 128)
    sides = (west, east)
    sibling = chip_id(x, y, 1 - core, z)
    x_ids = [chip_id((x + d) % 4, y, core, z) for d in (1, 2, 3)]
    y_ids = [chip_id(x, (y + d) % 4, core, z) for d in (1, 2, 3)]
    z_ids = [chip_id(x, y, core, (z + d) % 4) for d in (1, 2, 3)]

    loads = [
        pltpu.make_async_copy(node_h.at[pl.ds(0, LENT)], lent, load_sem.at[0]),
        pltpu.make_async_copy(node_h.at[pl.ds(LENT, LENT)], ext0.at[pl.ds(LENT, LENT)], load_sem.at[1]),
        pltpu.make_async_copy(adj_h, adj, load_sem.at[2]),
        pltpu.make_async_copy(wself_h.at[0], w_in.at[0, pl.ds(0, HID)], load_sem.at[3]),
        pltpu.make_async_copy(wself_h.at[1], w_in.at[1, pl.ds(0, HID)], load_sem.at[4]),
        pltpu.make_async_copy(wnbr_h.at[0], w_in.at[0, pl.ds(HID, HID)], load_sem.at[5]),
        pltpu.make_async_copy(wnbr_h.at[1], w_in.at[1, pl.ds(HID, HID)], load_sem.at[6]),
        pltpu.make_async_copy(wout_h, w_out, load_sem.at[7]),
        pltpu.make_async_copy(cot_h, cot, load_sem.at[8]),
    ]
    for copy in loads:
        copy.start()

    barrier = pltpu.get_barrier_semaphore()
    greeted = [west, east, sibling, *x_ids, *y_ids, *z_ids]
    for device in greeted:
        pl.semaphore_signal(barrier, inc=1, device_id=device, device_id_type=MESH)
    pl.semaphore_wait(barrier, len(greeted))

    def remote(src, dst, ssem, rsem, device):
        return pltpu.make_async_remote_copy(
            src_ref=src, dst_ref=dst, send_sem=ssem, recv_sem=rsem, device_id=device, device_id_type=MESH
        )

    def halo(n, src, dst, side, j):
        place = 40 + j if side == 0 else 32 + j
        return remote(src.at[side * 8 + j], dst.at[place], hs.at[n, side, j], hr.at[n, side, j], sides[side])

    def back(n, src, dst, side, j):
        place = 8 + j if side == 0 else j
        return remote(src.at[side * 8 + j], dst.at[place], hs.at[n, side, j], hr.at[n, side, j], sides[side])

    loads[0].wait()

    def give(j, c):
        for side in (0, 1):
            ext0[side * 8 + j] = lent[bound_s[0, side, j]]
            halo(0, ext0, ext0, side, j).start()
        return c

    lax.fori_loop(0, 8, give, 0)

    build_tables(nbr_v[...], bound_s, tab_v)
    tab_copy = pltpu.make_async_copy(tab_v, tab, tab_sem)
    tab_copy.start()
    for copy in loads[1:]:
        copy.wait()
    for s in (0, 1):
        w_out_t[s] = w_out[s].T
        w_self_t[s] = w_in[s, 0:HID].T
        w_nbr_t[s] = w_in[s, HID : 2 * HID].T
        total[s] = jnp.zeros((GRADS, HID), F32)

    def flip(t, c):
        for k in range(4):
            adj_t[t * 4 + k] = adj[t, k].T
        return c

    lax.fori_loop(0, NT, flip, 0)
    tab_copy.wait()
    live = live_s[0]

    def alive(q):
        return jnp.where(q < live, 1.0, 0.0).astype(F32)

    def cot_of(t, masked):
        c = cot[t]
        return (c.astype(F32) * alive(t)).astype(BF) if masked else c

    def tiles_of(group, i, count):
        if group:
            return [(LENT + i * count + n, LENT + i * count + n) for n in range(count)]
        half = count // 2
        return [
            (bound_s[0, side, i * half + n], side * 8 + i * half + n) for n in range(half) for side in (0, 1)
        ]

    def stacked(ref, tiles):
        return jnp.concatenate([ref[q] for _, q in tiles], axis=0)

    def put(ref, tiles, value):
        for n, (_, q) in enumerate(tiles):
            ref[q] = value[n * ROWS : (n + 1) * ROWS]

    def slope_up(group, i, c):
        tiles = tiles_of(group, i, 4)
        m = jnp.concatenate([cot_of(t, group) for t, _ in tiles], axis=0)
        put(scan, tiles, dot(m, w_out_t[1]))
        return c

    lax.fori_loop(0, 4, functools.partial(slope_up, 0), 0)
    lax.fori_loop(0, 4, functools.partial(slope_up, 1), 0)

    def gathered(ext, tiles):
        parts = []
        for t, _ in tiles:
            left = jnp.concatenate([adj[t, k] for k in range(4)], axis=1)
            right = jnp.concatenate([ext[tab[0, nbr_s[t, k]]] for k in range(4)], axis=0)
            parts.append(dot(left, right).astype(BF))
        return jnp.concatenate(parts, axis=0)

    def layer(s, ext, agg, act, tiles):
        f = stacked(ext, tiles)
        a = gathered(ext, tiles)
        put(agg, tiles, a)
        pre = dot(jnp.concatenate([f, a], axis=1), w_in[s]) + bias_v[s : s + 1, :]
        gate = 0.5 * jnp.tanh(0.5 * pre) + 0.5
        hidden = pre * gate
        h = hidden.astype(BF)
        put(act, tiles, h)
        return f, h, gate + hidden * (1.0 - gate)

    def masked_rows(group, tiles, value):
        if not group:
            return value
        return jnp.concatenate(
            [value[n * ROWS : (n + 1) * ROWS] * alive(t) for n, (t, _) in enumerate(tiles)], axis=0
        )

    def first(group, i, c):
        tiles = tiles_of(group, i, 2)
        f, h, slope = layer(0, ext0, agg0, act0, tiles)
        put(slope0, tiles, slope)
        out = masked_rows(group, tiles, f.astype(F32) + dot(h, w_out[0])).astype(BF)
        put(ext1, tiles, out)
        if not group:
            for side in (0, 1):
                halo(1, ext1, ext1, side, i).start()
        return c

    def land(n, ext, j, c):
        for side in (0, 1):
            halo(n, ext, ext, side, j).wait_recv()
        return c

    lax.fori_loop(0, 8, functools.partial(land, 0, ext0), 0)
    lax.fori_loop(0, 8, functools.partial(first, 0), 0)
    lax.fori_loop(0, 8, functools.partial(first, 1), 0)

    lax.fori_loop(0, 8, functools.partial(land, 1, ext1), 0)

    def second(group, i, c):
        tiles = tiles_of(group, i, 4)
        _, _, slope = layer(1, ext1, agg1, act1, tiles)
        d = (stacked(scan, tiles) * slope).astype(BF)
        put(dpre, tiles, d)
        put(dagg, tiles, dot(d, w_nbr_t[1]).astype(BF))
        return c

    lax.fori_loop(0, 4, functools.partial(second, 0), 0)
    lax.fori_loop(0, 4, functools.partial(second, 1), 0)

    def pair(r, c):
        i = tab[1, r]
        value = dot(adj_t[i], dagg[tab[0, i // 4]])
        earlier = scan[jnp.maximum(r - 1, 0)]
        scan[r] = value + jnp.where(tab[2, r] > 0, earlier, jnp.zeros_like(earlier))
        return c

    def pairs(begin, end):
        lax.fori_loop(begin, end, pair, 0)

    def collected(target):
        low = scan[tab[3, target]]
        high = scan[tab[5, target]]
        nil = jnp.zeros_like(low)
        return jnp.where(tab[4, target] > 0, low, nil) + jnp.where(tab[6, target] > 0, high, nil)

    def give_back(n, src, dst, j, c):
        for side in (0, 1):
            src[side * 8 + j] = collected(32 + side * 8 + j).astype(BF)
            back(n, src, dst, side, j).start()
        return c

    pairs(0, GROUP)
    pairs(GROUP, PAIRS)
    lax.fori_loop(0, 8, functools.partial(give_back, 2, send1, ret1), 0)

    def unlent(src, dst, t, c):
        dst[t] = src[tab[0, t]]
        return c

    lax.fori_loop(0, LENT, functools.partial(unlent, ext1, send0), 0)
    store_a = pltpu.make_async_copy(send0, out_h.at[0, pl.ds(0, LENT)], store_sem.at[0])
    store_b = pltpu.make_async_copy(ext1.at[pl.ds(LENT, LENT)], out_h.at[0, pl.ds(LENT, LENT)], store_sem.at[1])
    store_a.start()
    store_b.start()

    def straight(s, tiles, m):
        d = dot(stacked(dpre, tiles), w_self_t[s])
        parts = []
        for n, (t, q) in enumerate(tiles):
            own = dot(adj_t[t * 4], dagg[q]) + collected(t)
            parts.append(m[n * ROWS : (n + 1) * ROWS].astype(F32) + d[n * ROWS : (n + 1) * ROWS] + own)
        return jnp.concatenate(parts, axis=0)

    def add_grads(s, ext, agg, act, tiles, m):
        d = stacked(dpre, tiles)
        total[s, 0:HID] += dot_rows(stacked(ext, tiles), d)
        total[s, HID : 2 * HID] += dot_rows(stacked(agg, tiles), d)
        total[s, 2 * HID : 3 * HID] += dot_rows(stacked(act, tiles), m)
        total[s, 3 * HID : 3 * HID + 1] += jnp.sum(d.astype(F32), axis=0, keepdims=True)

    def later(group, i, c):
        tiles = tiles_of(group, i, 4)
        m = jnp.concatenate([cot_of(t, group) for t, _ in tiles], axis=0)
        add_grads(1, ext1, agg1, act1, tiles, m)
        value = straight(1, tiles, m)
        if group:
            put(mid, tiles, value.astype(BF))
        else:
            put(direct, tiles, value)
        return c

    lax.fori_loop(0, 4, functools.partial(later, 0), 0)
    lax.fori_loop(0, 4, functools.partial(later, 1), 0)

    def core_step(s):
        return remote(pack.at[s, pl.ds((1 - core) * 512, 512)], rc.at[s], gs.at[s, 0, 0], gr.at[s, 0, 0], sibling)

    def x_step(s, d):
        rows = pl.ds(core * 512 + ((x + d) % 4) * 128, 128)
        return remote(pack.at[s, rows], rx.at[s, d - 1], gs.at[s, 1, d - 1], gr.at[s, 1, d - 1], x_ids[d - 1])

    def y_step(s, d):
        rows = pl.ds(core * 512 + x * 128 + ((y + d) % 4) * 32, 32)
        return remote(pack.at[s, rows], ry.at[s, d - 1], gs.at[s, 2, d - 1], gr.at[s, 2, d - 1], y_ids[d - 1])

    def z_step(s, d):
        return remote(rz.at[s, z], rz.at[s, z], gs.at[s, 3, d - 1], gr.at[s, 3, d - 1], z_ids[d - 1])

    def spread_step(s, level, d):
        base, size = (
            (core * 512 + x * 128 + y * 32, 32),
            (core * 512 + x * 128, 128),
            (core * 512, 512),
        )[level]
        rows = full.at[s, pl.ds(base, size)]
        device = (y_ids, x_ids, [sibling])[level][d - 1]
        return remote(rows, rows, gs.at[s, 4 + level, d - 1], gr.at[s, 4 + level, d - 1], device)

    def sums_begin(s):
        other = pl.ds((1 - core) * 512, 512)
        pack[s, other] = total[s, other].astype(BF)
        core_step(s).start()

    def sums_x(s):
        core_step(s).wait_recv()
        own = pl.ds(core * 512, 512)
        value = total[s, own] + rc[s].astype(F32)
        total[s, own] = value
        pack[s, own] = value.astype(BF)
        for d in (1, 2, 3):
            x_step(s, d).start()

    def sums_y(s):
        for d in (1, 2, 3):
            x_step(s, d).wait()
        own = pl.ds(core * 512 + x * 128, 128)
        value = total[s, own] + rx[s, 0].astype(F32) + rx[s, 1].astype(F32) + rx[s, 2].astype(F32)
        total[s, own] = value
        pack[s, own] = value.astype(BF)
        for d in (1, 2, 3):
            y_step(s, d).start()

    def sums_z(s):
        for d in (1, 2, 3):
            y_step(s, d).wait_recv()
        own = pl.ds(core * 512 + x * 128 + y * 32, 32)
        value = total[s, own] + ry[s, 0].astype(F32) + ry[s, 1].astype(F32) + ry[s, 2].astype(F32)
        rz[s, z] = value.astype(BF)
        for d in (1, 2, 3):
            z_step(s, d).start()

    def z_landed(s, d):
        src = rz.at[s, (z + 4 - d) % 4]
        return remote(src, src, gs.at[s, 3, d - 1], gr.at[s, 3, d - 1], z_ids[d - 1])

    def sums_back(s):
        for d in (1, 2, 3):
            z_landed(s, d).wait_recv()
        value = rz[s, 0].astype(F32) + rz[s, 1].astype(F32) + rz[s, 2].astype(F32) + rz[s, 3].astype(F32)
        full[s, pl.ds(core * 512 + x * 128 + y * 32, 32)] = value.astype(BF)
        for d in (1, 2, 3):
            spread_step(s, 0, d).start()

    def landed(s, level, d):
        base, size = (
            (core * 512 + x * 128 + ((y + 4 - d) % 4) * 32, 32),
            (core * 512 + ((x + 4 - d) % 4) * 128, 128),
            ((1 - core) * 512, 512),
        )[level]
        rows = full.at[s, pl.ds(base, size)]
        return remote(rows, rows, gs.at[s, 4 + level, d - 1], gr.at[s, 4 + level, d - 1], sibling)

    def sums_up(s, level):
        for d in (1, 2, 3):
            landed(s, level, d).wait_recv()
        for d in (1, 2, 3) if level == 0 else (1,):
            spread_step(s, level + 1, d).start()

    def sums_end(s):
        landed(s, 2, 1).wait_recv()
        store = pltpu.make_async_copy(full.at[s], sums_h.at[s], store_sem.at[6 + s])
        store.start()
        return store

    sums_begin(1)

    def last_out(i, c):
        ts = [i * 4 + n for n in range(4)]
        qs = [tab[0, t] for t in ts]
        h = jnp.concatenate([act1[q] for q in qs], axis=0)
        f = jnp.concatenate([ext1[q] for q in qs], axis=0)
        value = f.astype(F32) + dot(h, w_out[1])
        for n, t in enumerate(ts):
            cot[t] = (value[n * ROWS : (n + 1) * ROWS] * alive(t)).astype(BF)
        return c

    def pull(tiles, m):
        d = (dot(m, w_out_t[0]) * stacked(slope0, tiles)).astype(BF)
        put(dpre, tiles, d)
        put(dagg, tiles, dot(d, w_nbr_t[0]).astype(BF))

    def early_rest(i, c):
        tiles = tiles_of(1, i, 4)
        m = jnp.concatenate([(mid[q].astype(F32) * alive(t)).astype(BF) for t, q in tiles], axis=0)
        pull(tiles, m)
        add_grads(0, ext0, agg0, act0, tiles, m)
        return c

    lax.fori_loop(0, 4, early_rest, 0)
    pairs(0, GROUP)
    sums_x(1)
    lax.fori_loop(0, 8, last_out, 0)
    store_c = pltpu.make_async_copy(cot, out_h.at[1], store_sem.at[2])
    store_c.start()
    store_d = pltpu.make_async_copy(mid.at[pl.ds(LENT, LENT)], grad_h.at[1, pl.ds(LENT, LENT)], store_sem.at[3])
    store_d.start()
    sums_y(1)

    def early(i, c):
        for side in (0, 1):
            back(2, send1, ret1, side, i).wait_recv()
        tiles = tiles_of(0, i, 2)
        m = (stacked(direct, tiles) + stacked(ret1, tiles).astype(F32)).astype(BF)
        put(mid, tiles, m)
        pull(tiles, m)
        add_grads(0, ext0, agg0, act0, tiles, m)
        return c

    lax.fori_loop(0, 8, early, 0)
    sums_begin(0)
    sums_z(1)
    store_a.wait()
    pairs(GROUP, PAIRS)
    lax.fori_loop(0, 8, functools.partial(give_back, 3, send0, ret0), 0)
    sums_x(0)
    sums_back(1)

    lax.fori_loop(0, LENT, functools.partial(unlent, mid, lent), 0)
    store_e = pltpu.make_async_copy(lent, grad_h.at[1, pl.ds(0, LENT)], store_sem.at[4])
    store_e.start()

    def whole(group, i, c):
        tiles = tiles_of(group, i, 4)
        if group:
            m = jnp.concatenate([(mid[q].astype(F32) * alive(t)).astype(BF) for t, q in tiles], axis=0)
            put(act1, tiles, straight(0, tiles, m).astype(BF))
        else:
            put(direct, tiles, straight(0, tiles, stacked(mid, tiles)))
        return c

    lax.fori_loop(0, 4, functools.partial(whole, 1), 0)
    sums_y(0)
    sums_up(1, 0)
    lax.fori_loop(0, 4, functools.partial(whole, 0), 0)
    store_f = pltpu.make_async_copy(act1.at[pl.ds(LENT, LENT)], grad_h.at[0, pl.ds(LENT, LENT)], store_sem.at[5])
    store_f.start()
    sums_z(0)
    sums_up(1, 1)

    def arrive(j, c):
        for side in (0, 1):
            back(3, send0, ret0, side, j).wait_recv()
        return c

    lax.fori_loop(0, 8, arrive, 0)
    sums_back(0)

    def finish(t, c):
        q = tab[0, t]
        act1[t] = (direct[q] + ret0[q].astype(F32)).astype(BF)
        return c

    lax.fori_loop(0, LENT, finish, 0)
    store_g = pltpu.make_async_copy(act1.at[pl.ds(0, LENT)], grad_h.at[0, pl.ds(0, LENT)], store_sem.at[0])
    store_g.start()
    store_h = sums_end(1)
    sums_up(0, 0)
    sums_up(0, 1)
    store_i = sums_end(0)

    def drain(j, c):
        for side in (0, 1):
            halo(0, ext0, ext0, side, j).wait_send()
            halo(1, ext1, ext1, side, j).wait_send()
            back(2, send1, ret1, side, j).wait_send()
            back(3, send0, ret0, side, j).wait_send()
        return c

    lax.fori_loop(0, 8, drain, 0)
    for s in (1, 0):
        core_step(s).wait_send()
        for d in (1, 2, 3):
            y_step(s, d).wait_send()
            z_step(s, d).wait_send()
            spread_step(s, 0, d).wait_send()
            spread_step(s, 1, d).wait_send()
        spread_step(s, 2, 1).wait_send()
    for copy in (store_b, store_c, store_d, store_e, store_f, store_g, store_h, store_i):
        copy.wait()


def per_device(
    node_in, out_cot, adjacency, tile_nbrs, bound_tiles, live_tiles, w_self, w_nbr, pre_bias, w_out
):
    anyspace = pl.BlockSpec(memory_space=pl.ANY)
    vmem = pl.BlockSpec(memory_space=pltpu.VMEM)
    smem = pl.BlockSpec(memory_space=pltpu.SMEM)
    tiles = lambda n, dtype=BF: pltpu.VMEM((n, ROWS, HID), dtype)
    dma = pltpu.SemaphoreType.DMA
    scratch = [
        pltpu.VMEM((NT, 4, ROWS, ROWS), BF),
        pltpu.VMEM((NT * 4, ROWS, ROWS), BF),
        tiles(NT),
        tiles(LENT),
        tiles(48),
        tiles(48),
        tiles(NT),
        tiles(NT),
        tiles(NT),
        tiles(NT),
        tiles(NT, F32),
        tiles(NT),
        tiles(NT),
        tiles(PAIRS, F32),
        tiles(LENT, F32),
        tiles(NT),
        tiles(LENT),
        tiles(LENT),
        tiles(LENT),
        tiles(LENT),
        pltpu.VMEM((2, 2 * HID, HID), BF),
        pltpu.VMEM((2, HID, HID), BF),
        pltpu.VMEM((2, HID, HID), BF),
        pltpu.VMEM((2, HID, HID), BF),
        pltpu.VMEM((2, HID, HID), BF),
        pltpu.VMEM((2, GRADS, HID), F32),
        pltpu.VMEM((2, GRADS, HID), BF),
        pltpu.VMEM((2, 512, HID), BF),
        pltpu.VMEM((2, 3, 128, HID), BF),
        pltpu.VMEM((2, 3, 32, HID), BF),
        pltpu.VMEM((2, 4, 32, HID), BF),
        pltpu.VMEM((2, GRADS, HID), BF),
        pltpu.VMEM((8, 128), jnp.int32),
        pltpu.SMEM((8, 128), jnp.int32),
        dma((9,)),
        dma,
        dma((8,)),
        dma((4, 2, 8)),
        dma((4, 2, 8)),
        dma((2, 7, 3)),
        dma((2, 7, 3)),
    ]
    out, grad, sums = pl.pallas_call(
        mega,
        out_shape=(
            jax.ShapeDtypeStruct((2, NT, ROWS, HID), BF),
            jax.ShapeDtypeStruct((2, NT, ROWS, HID), BF),
            jax.ShapeDtypeStruct((2, GRADS, HID), BF),
        ),
        in_specs=[
            anyspace, anyspace, anyspace, vmem, smem, smem, smem, anyspace, anyspace, vmem, anyspace,
        ],
        out_specs=(anyspace, anyspace, anyspace),
        scratch_shapes=scratch,
        compiler_params=pltpu.CompilerParams(
            collective_id=0, has_side_effects=True, vmem_limit_bytes=67043328
        ),
        name="mesh_layers",
    )(
        node_in.reshape(NT, ROWS, HID), out_cot.reshape(NT, ROWS, HID), adjacency,
        tile_nbrs, tile_nbrs, bound_tiles, live_tiles, w_self, w_nbr, pre_bias, w_out,
    )
    rows = NT * ROWS
    grad_sums = sums.astype(F32)
    return (
        out.reshape(2, rows, HID),
        grad.reshape(2, rows, HID),
        grad_sums[:, 0:HID],
        grad_sums[:, HID : 2 * HID],
        grad_sums[:, 3 * HID],
        grad_sums[:, 2 * HID : 3 * HID],
    )


def solution(mesh):
    split = P(AXES)
    in_specs = (split,) * 6 + (P(),) * 4
    out_specs = (P(None, AXES), P(None, AXES), P(), P(), P(), P())
    return jax.shard_map(
        per_device, mesh=mesh, in_specs=in_specs, out_specs=out_specs, check_vma=False
    )
```

```python
import functools

import jax
import jax.numpy as jnp
from jax import lax
from jax.experimental import pallas as pl
from jax.experimental.pallas import tpu as pltpu
from jax.sharding import PartitionSpec as P

AXES = ("dom", "phase", "feat")
MESH = pl.DeviceIdType.MESH
BF = jnp.bfloat16
F32 = jnp.float32
NT = 32
LENT = 16
ROWS = 128
HID = 256
PAIRS = 96
GROUP = 48
GRADS = 1024
UNROLL = 8
AHEAD = 2


def dot(a, b):
    return lax.dot_general(a, b, (((1,), (0,)), ((), ())), preferred_element_type=F32)


def dot_rows(a, b):
    return lax.dot_general(a, b, (((0,), (0,)), ((), ())), preferred_element_type=F32)


def chip_id(x, y, core, z):
    return (x * 4 + (y // 2) * 2 + core, y % 2, z)


def part_id(part):
    return (part // 8, (part // 4) % 2, part % 4)


def build_tables(nbr_vec, bound_sm, tab_v):
    i32 = jnp.int32
    lane32 = lax.broadcasted_iota(i32, (NT, 128), 1)
    row32 = lax.broadcasted_iota(i32, (NT, 128), 0)
    square = lax.broadcasted_iota(i32, (NT, NT), 0) == lax.broadcasted_iota(i32, (NT, NT), 1)
    spread = jnp.zeros((NT, 128), i32)
    for k in range(4):
        line = jnp.broadcast_to(nbr_vec[k : k + 1, :], (NT, NT))
        column = jnp.sum(jnp.where(square, line, 0), axis=1, keepdims=True)
        here = (lane32 // 4 == row32) & (lane32 % 4 == k)
        spread = spread + jnp.where(here, jnp.broadcast_to(column, (NT, 128)), 0)
    target = jnp.sum(spread, axis=0, keepdims=True)
    lane = lax.broadcasted_iota(i32, (1, 128), 1)
    key = jnp.where(lane % 4 == 0, 4096, jnp.where(lane // 4 < LENT, 256, 0) + target)
    li = lax.broadcasted_iota(i32, (128, 128), 1)
    ri = lax.broadcasted_iota(i32, (128, 128), 0)
    key_l = jnp.broadcast_to(key, (128, 128))
    key_c = jnp.sum(jnp.where(li == ri, key_l, 0), axis=1, keepdims=True)
    key_r = jnp.broadcast_to(key_c, (128, 128))
    before = (key_l < key_r) | ((key_l == key_r) & (li < ri))
    rank = jnp.sum(jnp.where(before, 1, 0), axis=1, keepdims=True)
    same = jnp.sum(jnp.where((key_l == key_r) & (li < ri), 1, 0), axis=1, keepdims=True)
    place = jnp.broadcast_to(rank, (128, 128)) == li
    order = jnp.sum(jnp.where(place, ri, 0), axis=0, keepdims=True)
    joins = jnp.sum(jnp.where(place, jnp.broadcast_to(same, (128, 128)), 0), axis=0, keepdims=True)
    slot = lane
    for q in range(LENT):
        slot = jnp.where(lane == bound_sm[0, q // 8, q % 8], q, slot)
    rows = [slot, order, joins]
    for base in (0, 256):
        upto = jnp.sum(jnp.where(key_r <= li + base, 1, 0), axis=0, keepdims=True) - 1
        rows.append(jnp.maximum(upto, 0))
        rows.append(jnp.sum(jnp.where(key_r == li + base, 1, 0), axis=0, keepdims=True))
    for n, row in enumerate(rows):
        tab_v[n : n + 1, :] = row


def mega(
    node_h, cot_h, adj_h, nbr_v, nbr_s, bound_s, live_s, wself_h, wnbr_h, bias_v, wout_h,
    out_h, grad_h, sums_h,
    adj, adj_t, cot, lent, ext0, ext1, agg0, agg1, act0, act1, slope0, dpre, dagg, scan, direct, mid,
    ret1, ret0, send1, send0, w_in, w_out, w_out_t, w_self_t, w_nbr_t,
    total, pack, rc, rx, ry, rz, full, tab_v, tab,
    load_sem, tab_sem, store_sem, hs, hr, gs, gr,
):
    dom, phase, feat = (lax.axis_index(a) for a in AXES)
    x, core = dom // 4, dom % 2
    y = ((dom // 2) % 2) * 2 + phase
    z = feat
    part = dom * 8 + phase * 4 + feat
    west = part_id((part + 127) % 128)
    east = part_id((part + 1) % 128)
    sides = (west, east)
    sibling = chip_id(x, y, 1 - core, z)
    x_ids = [chip_id((x + d) % 4, y, core, z) for d in (1, 2, 3)]
    y_ids = [chip_id(x, (y + d) % 4, core, z) for d in (1, 2, 3)]
    z_ids = [chip_id(x, y, core, (z + d) % 4) for d in (1, 2, 3)]

    loads = [
        pltpu.make_async_copy(node_h.at[pl.ds(0, LENT)], lent, load_sem.at[0]),
        pltpu.make_async_copy(node_h.at[pl.ds(LENT, LENT)], ext0.at[pl.ds(LENT, LENT)], load_sem.at[1]),
        pltpu.make_async_copy(adj_h, adj, load_sem.at[2]),
        pltpu.make_async_copy(wself_h.at[0], w_in.at[0, pl.ds(0, HID)], load_sem.at[3]),
        pltpu.make_async_copy(wself_h.at[1], w_in.at[1, pl.ds(0, HID)], load_sem.at[4]),
        pltpu.make_async_copy(wnbr_h.at[0], w_in.at[0, pl.ds(HID, HID)], load_sem.at[5]),
        pltpu.make_async_copy(wnbr_h.at[1], w_in.at[1, pl.ds(HID, HID)], load_sem.at[6]),
        pltpu.make_async_copy(wout_h, w_out, load_sem.at[7]),
        pltpu.make_async_copy(cot_h, cot, load_sem.at[8]),
    ]
    for copy in loads:
        copy.start()

    barrier = pltpu.get_barrier_semaphore()
    greeted = [west, east, sibling, *x_ids, *y_ids, *z_ids]
    for device in greeted:
        pl.semaphore_signal(barrier, inc=1, device_id=device, device_id_type=MESH)
    pl.semaphore_wait(barrier, len(greeted))

    def remote(src, dst, ssem, rsem, device):
        return pltpu.make_async_remote_copy(
            src_ref=src, dst_ref=dst, send_sem=ssem, recv_sem=rsem, device_id=device, device_id_type=MESH
        )

    def halo(n, src, dst, side, j):
        place = 40 + j if side == 0 else 32 + j
        return remote(src.at[side * 8 + j], dst.at[place], hs.at[n, side, j], hr.at[n, side, j], sides[side])

    def back(n, src, dst, side, j):
        place = 8 + j if side == 0 else j
        return remote(src.at[side * 8 + j], dst.at[place], hs.at[n, side, j], hr.at[n, side, j], sides[side])

    loads[0].wait()

    def give(j, c):
        for side in (0, 1):
            ext0[side * 8 + j] = lent[bound_s[0, side, j]]
            halo(0, ext0, ext0, side, j).start()
        return c

    lax.fori_loop(0, 8, give, 0)

    build_tables(nbr_v[...], bound_s, tab_v)
    tab_copy = pltpu.make_async_copy(tab_v, tab, tab_sem)
    tab_copy.start()
    for copy in loads[1:]:
        copy.wait()
    for s in (0, 1):
        w_out_t[s] = w_out[s].T
        w_self_t[s] = w_in[s, 0:HID].T
        w_nbr_t[s] = w_in[s, HID : 2 * HID].T
        total[s] = jnp.zeros((GRADS, HID), F32)

    tab_copy.wait()
    live = live_s[0]

    def alive(q):
        return jnp.where(q < live, 1.0, 0.0).astype(F32)

    def cot_of(t, masked):
        c = cot[t]
        return (c.astype(F32) * alive(t)).astype(BF) if masked else c

    def tiles_of(group, i, count):
        if group:
            return [(LENT + i * count + n, LENT + i * count + n) for n in range(count)]
        half = count // 2
        return [
            (bound_s[0, side, i * half + n], side * 8 + i * half + n) for n in range(half) for side in (0, 1)
        ]

    def stacked(ref, tiles):
        return jnp.concatenate([ref[q] for _, q in tiles], axis=0)

    def put(ref, tiles, value):
        for n, (_, q) in enumerate(tiles):
            ref[q] = value[n * ROWS : (n + 1) * ROWS]

    def slope_up(group, i, c):
        tiles = tiles_of(group, i, 4)
        m = jnp.concatenate([cot_of(t, group) for t, _ in tiles], axis=0)
        put(scan, tiles, dot(m, w_out_t[1]))
        return c

    def gathered(ext, tiles):
        parts = []
        for t, _ in tiles:
            left = jnp.concatenate([adj[t, k] for k in range(4)], axis=1)
            right = jnp.concatenate([ext[tab[0, nbr_s[k, t]]] for k in range(4)], axis=0)
            parts.append(dot(left, right).astype(BF))
        return jnp.concatenate(parts, axis=0)

    def layer(s, ext, agg, act, tiles):
        f = stacked(ext, tiles)
        a = gathered(ext, tiles)
        put(agg, tiles, a)
        pre = dot(jnp.concatenate([f, a], axis=1), w_in[s]) + bias_v[s : s + 1, :]
        gate = 0.5 * jnp.tanh(0.5 * pre) + 0.5
        hidden = pre * gate
        h = hidden.astype(BF)
        put(act, tiles, h)
        return f, h, gate + hidden * (1.0 - gate)

    def masked_rows(group, tiles, value):
        if not group:
            return value
        return jnp.concatenate(
            [value[n * ROWS : (n + 1) * ROWS] * alive(t) for n, (t, _) in enumerate(tiles)], axis=0
        )

    def first(group, i, c):
        tiles = tiles_of(group, i, 2)
        f, h, slope = layer(0, ext0, agg0, act0, tiles)
        put(slope0, tiles, slope)
        out = masked_rows(group, tiles, f.astype(F32) + dot(h, w_out[0])).astype(BF)
        put(ext1, tiles, out)
        if not group:
            for side in (0, 1):
                halo(1, ext1, ext1, side, i).start()
        return c

    def land(n, ext, j, c):
        for side in (0, 1):
            halo(n, ext, ext, side, j).wait_recv()
        return c

    lax.fori_loop(0, 8, functools.partial(land, 0, ext0), 0)
    lax.fori_loop(0, 8, functools.partial(first, 0), 0)
    lax.fori_loop(0, 8, functools.partial(first, 1), 0)
    lax.fori_loop(0, 4, functools.partial(slope_up, 0), 0)
    lax.fori_loop(0, 4, functools.partial(slope_up, 1), 0)

    def flip(t, c):
        for k in range(4):
            adj_t[t * 4 + k] = adj[t, k].T
        return c

    lax.fori_loop(0, NT, flip, 0)

    lax.fori_loop(0, 8, functools.partial(land, 1, ext1), 0)

    def second(group, i, c):
        tiles = tiles_of(group, i, 4)
        _, _, slope = layer(1, ext1, agg1, act1, tiles)
        d = (stacked(scan, tiles) * slope).astype(BF)
        put(dpre, tiles, d)
        put(dagg, tiles, dot(d, w_nbr_t[1]).astype(BF))
        return c

    lax.fori_loop(0, 4, functools.partial(second, 0), 0)
    lax.fori_loop(0, 4, functools.partial(second, 1), 0)

    def pair(base, i, c):
        begin = base + i * UNROLL
        total_so_far = scan[jnp.maximum(begin - 1, 0)]
        for n in range(UNROLL):
            p = tab[1, begin + n]
            value = dot(adj_t[p], dagg[tab[0, p // 4]])
            keep = tab[2, begin + n] > 0
            total_so_far = value + jnp.where(keep, total_so_far, jnp.zeros_like(value))
            scan[begin + n] = total_so_far
        return c

    def pairs(begin, end):
        lax.fori_loop(0, (end - begin) // UNROLL, functools.partial(pair, begin), 0)

    def collected(target):
        low = scan[tab[3, target]]
        high = scan[tab[5, target]]
        nil = jnp.zeros_like(low)
        return jnp.where(tab[4, target] > 0, low, nil) + jnp.where(tab[6, target] > 0, high, nil)

    def give_back(n, src, dst, j, c):
        for side in (0, 1):
            src[side * 8 + j] = collected(32 + side * 8 + j).astype(BF)
            back(n, src, dst, side, j).start()
        return c

    pairs(0, GROUP)
    pairs(GROUP, PAIRS)
    lax.fori_loop(0, 8, functools.partial(give_back, 2, send1, ret1), 0)

    def unlent(src, dst, t, c):
        dst[t] = src[tab[0, t]]
        return c

    lax.fori_loop(0, LENT, functools.partial(unlent, ext1, send0), 0)
    store_a = pltpu.make_async_copy(send0, out_h.at[0, pl.ds(0, LENT)], store_sem.at[0])
    store_b = pltpu.make_async_copy(ext1.at[pl.ds(LENT, LENT)], out_h.at[0, pl.ds(LENT, LENT)], store_sem.at[1])
    store_a.start()
    store_b.start()

    def straight(s, tiles, m):
        d = dot(stacked(dpre, tiles), w_self_t[s])
        parts = []
        for n, (t, q) in enumerate(tiles):
            own = dot(adj_t[t * 4], dagg[q]) + collected(t)
            parts.append(m[n * ROWS : (n + 1) * ROWS].astype(F32) + d[n * ROWS : (n + 1) * ROWS] + own)
        return jnp.concatenate(parts, axis=0)

    def add_grads(s, ext, agg, act, tiles, m):
        d = stacked(dpre, tiles)
        total[s, 0:HID] += dot_rows(stacked(ext, tiles), d)
        total[s, HID : 2 * HID] += dot_rows(stacked(agg, tiles), d)
        total[s, 2 * HID : 3 * HID] += dot_rows(stacked(act, tiles), m)
        total[s, 3 * HID : 3 * HID + 1] += jnp.sum(d.astype(F32), axis=0, keepdims=True)

    def later_grads(group, i, c):
        tiles = tiles_of(group, i, 4)
        m = jnp.concatenate([cot_of(t, group) for t, _ in tiles], axis=0)
        add_grads(1, ext1, agg1, act1, tiles, m)
        return c

    def later(group, i, c):
        tiles = tiles_of(group, i, 4)
        m = jnp.concatenate([cot_of(t, group) for t, _ in tiles], axis=0)
        value = straight(1, tiles, m)
        if group:
            put(mid, tiles, value.astype(BF))
        else:
            put(direct, tiles, value)
        return c

    def core_step(s):
        return remote(pack.at[s, pl.ds((1 - core) * 512, 512)], rc.at[s], gs.at[s, 0, 0, 0], gr.at[s, 0, 0, 0], sibling)

    def order_of(h):
        return ((x, x_ids), (y, y_ids)) if h == 0 else ((y, y_ids), (x, x_ids))

    def columns(h):
        return pl.ds(h * 128, 128)

    def one_step(s, h, d):
        (p, ids), _ = order_of(h)
        rows = pl.ds(core * 512 + ((p + d) % 4) * 128, 128)
        src = pack.at[s, rows, columns(h)]
        return remote(src, rx.at[s, h, d - 1], gs.at[s, h, 1, d - 1], gr.at[s, h, 1, d - 1], ids[d - 1])

    def two_step(s, h, d):
        (p, _), (q, ids) = order_of(h)
        rows = pl.ds(core * 512 + p * 128 + ((q + d) % 4) * 32, 32)
        src = pack.at[s, rows, columns(h)]
        return remote(src, ry.at[s, h, d - 1], gs.at[s, h, 2, d - 1], gr.at[s, h, 2, d - 1], ids[d - 1])

    def z_step(s, d, slot):
        here = rz.at[s, slot]
        return remote(here, here, gs.at[s, 0, 3, d - 1], gr.at[s, 0, 3, d - 1], z_ids[d - 1])

    def spread_step(s, h, level, d, back_by=0):
        (p, ids_p), (q, ids_q) = order_of(h)
        if level == 0:
            base, size, ids = core * 512 + p * 128 + ((q + 4 - back_by) % 4) * 32, 32, ids_q
        else:
            base, size, ids = core * 512 + ((p + 4 - back_by) % 4) * 128, 128, ids_p
        rows = full.at[s, pl.ds(base, size), columns(h)]
        return remote(rows, rows, gs.at[s, h, 4 + level, d - 1], gr.at[s, h, 4 + level, d - 1], ids[d - 1])

    def half_step(s, half):
        rows = full.at[s, pl.ds(half * 512, 512)]
        return remote(rows, rows, gs.at[s, 0, 6, 0], gr.at[s, 0, 6, 0], sibling)

    def sums_begin(s):
        other = pl.ds((1 - core) * 512, 512)
        pack[s, other] = total[s, other].astype(BF)
        core_step(s).start()

    def sums_x(s):
        core_step(s).wait_recv()
        own = pl.ds(core * 512, 512)
        value = total[s, own] + rc[s].astype(F32)
        total[s, own] = value
        pack[s, own] = value.astype(BF)
        for d in (1, 2, 3):
            for h in (0, 1):
                one_step(s, h, d).start()

    def sums_y(s):
        for h in (0, 1):
            (p, _), _ = order_of(h)
            for d in (1, 2, 3):
                one_step(s, h, d).wait()
            own, cols = pl.ds(core * 512 + p * 128, 128), columns(h)
            value = total[s, own, cols]
            for d in (1, 2, 3):
                value = value + rx[s, h, d - 1].astype(F32)
            total[s, own, cols] = value
            pack[s, own, cols] = value.astype(BF)
            for d in (1, 2, 3):
                two_step(s, h, d).start()

    def sums_z(s):
        for h in (0, 1):
            (p, _), (q, _) = order_of(h)
            for d in (1, 2, 3):
                two_step(s, h, d).wait_recv()
            own = pl.ds(core * 512 + p * 128 + q * 32, 32)
            value = total[s, own, columns(h)]
            for d in (1, 2, 3):
                value = value + ry[s, h, d - 1].astype(F32)
            rz[s, z, h] = value.astype(BF)
        for d in (1, 2, 3):
            z_step(s, d, z).start()

    def sums_back(s):
        for d in (1, 2, 3):
            z_step(s, d, (z + 4 - d) % 4).wait_recv()
        for h in (0, 1):
            (p, _), (q, _) = order_of(h)
            value = rz[s, 0, h].astype(F32)
            for n in (1, 2, 3):
                value = value + rz[s, n, h].astype(F32)
            full[s, pl.ds(core * 512 + p * 128 + q * 32, 32), columns(h)] = value.astype(BF)
            for d in (1, 2, 3):
                spread_step(s, h, 0, d).start()

    def sums_up(s, level):
        for h in (0, 1):
            for d in (1, 2, 3):
                spread_step(s, h, level, d, d).wait_recv()
            if level == 0:
                for d in (1, 2, 3):
                    spread_step(s, h, 1, d).start()
        if level == 1:
            half_step(s, core).start()

    def sums_end(s):
        half_step(s, 1 - core).wait_recv()
        store = pltpu.make_async_copy(full.at[s], sums_h.at[s], store_sem.at[6 + s])
        store.start()
        return store

    lax.fori_loop(0, 4, functools.partial(later_grads, 0), 0)
    lax.fori_loop(0, 4, functools.partial(later_grads, 1), 0)
    sums_begin(1)
    lax.fori_loop(0, 4, functools.partial(later, 0), 0)
    lax.fori_loop(0, 4, functools.partial(later, 1), 0)
    sums_x(1)

    def last_out(i, c):
        ts = [i * 4 + n for n in range(4)]
        qs = [tab[0, t] for t in ts]
        h = jnp.concatenate([act1[q] for q in qs], axis=0)
        f = jnp.concatenate([ext1[q] for q in qs], axis=0)
        value = f.astype(F32) + dot(h, w_out[1])
        for n, t in enumerate(ts):
            cot[t] = (value[n * ROWS : (n + 1) * ROWS] * alive(t)).astype(BF)
        return c

    def pull(tiles, m):
        d = (dot(m, w_out_t[0]) * stacked(slope0, tiles)).astype(BF)
        put(dpre, tiles, d)
        put(dagg, tiles, dot(d, w_nbr_t[0]).astype(BF))

    def early_rest(i, c):
        tiles = tiles_of(1, i, 4)
        m = jnp.concatenate([(mid[q].astype(F32) * alive(t)).astype(BF) for t, q in tiles], axis=0)
        pull(tiles, m)
        add_grads(0, ext0, agg0, act0, tiles, m)
        return c

    lax.fori_loop(0, 4, early_rest, 0)
    pairs(0, GROUP)
    lax.fori_loop(0, 8, last_out, 0)
    store_c = pltpu.make_async_copy(cot, out_h.at[1], store_sem.at[2])
    store_c.start()
    store_d = pltpu.make_async_copy(mid.at[pl.ds(LENT, LENT)], grad_h.at[1, pl.ds(LENT, LENT)], store_sem.at[3])
    store_d.start()

    def early(i, c):
        for side in (0, 1):
            back(2, send1, ret1, side, i).wait_recv()
        tiles = tiles_of(0, i, 2)
        m = (stacked(direct, tiles) + stacked(ret1, tiles).astype(F32)).astype(BF)
        put(mid, tiles, m)
        pull(tiles, m)
        add_grads(0, ext0, agg0, act0, tiles, m)
        return c

    lax.fori_loop(0, 8, early, 0)
    sums_begin(0)
    sums_y(1)
    store_a.wait()
    pairs(GROUP, PAIRS)

    def hold_back(j, c):
        for side in (0, 1):
            send0[side * 8 + j] = collected(32 + side * 8 + j).astype(BF)
        return c

    def in_turn(j, c):
        for side in (0, 1):
            back(3, send0, ret0, side, j - AHEAD).wait_send()
            back(3, send0, ret0, side, j).start()
        return c

    lax.fori_loop(0, AHEAD, functools.partial(give_back, 3, send0, ret0), 0)
    sums_x(0)
    lax.fori_loop(AHEAD, 8, hold_back, 0)
    sums_z(1)

    lax.fori_loop(0, LENT, functools.partial(unlent, mid, lent), 0)
    store_e = pltpu.make_async_copy(lent, grad_h.at[1, pl.ds(0, LENT)], store_sem.at[4])
    store_e.start()

    def whole(group, i, c):
        tiles = tiles_of(group, i, 4)
        if group:
            m = jnp.concatenate([(mid[q].astype(F32) * alive(t)).astype(BF) for t, q in tiles], axis=0)
            put(act1, tiles, straight(0, tiles, m).astype(BF))
        else:
            put(direct, tiles, straight(0, tiles, stacked(mid, tiles)))
        return c

    lax.fori_loop(0, 2, functools.partial(whole, 1), 0)
    lax.fori_loop(AHEAD, 4, in_turn, 0)
    sums_back(1)
    sums_y(0)
    lax.fori_loop(4, 6, in_turn, 0)
    lax.fori_loop(2, 4, functools.partial(whole, 1), 0)
    store_f = pltpu.make_async_copy(act1.at[pl.ds(LENT, LENT)], grad_h.at[0, pl.ds(LENT, LENT)], store_sem.at[5])
    store_f.start()
    sums_up(1, 0)
    sums_z(0)
    lax.fori_loop(6, 8, in_turn, 0)
    lax.fori_loop(0, 4, functools.partial(whole, 0), 0)
    sums_up(1, 1)
    sums_back(0)
    sums_up(0, 0)

    def arrive(j, c):
        for side in (0, 1):
            back(3, send0, ret0, side, j).wait_recv()
        return c

    lax.fori_loop(0, 8, arrive, 0)

    def finish(t, c):
        q = tab[0, t]
        act1[t] = (direct[q] + ret0[q].astype(F32)).astype(BF)
        return c

    lax.fori_loop(0, LENT, finish, 0)
    store_g = pltpu.make_async_copy(act1.at[pl.ds(0, LENT)], grad_h.at[0, pl.ds(0, LENT)], store_sem.at[0])
    store_g.start()
    store_h = sums_end(1)
    sums_up(0, 1)
    store_i = sums_end(0)

    def drain(j, c):
        for side in (0, 1):
            halo(0, ext0, ext0, side, j).wait_send()
            halo(1, ext1, ext1, side, j).wait_send()
            back(2, send1, ret1, side, j).wait_send()
        return c

    def drain_last(j, c):
        for side in (0, 1):
            back(3, send0, ret0, side, j).wait_send()
        return c

    lax.fori_loop(0, 8, drain, 0)
    lax.fori_loop(8 - AHEAD, 8, drain_last, 0)
    for s in (1, 0):
        core_step(s).wait_send()
        half_step(s, core).wait_send()
        for d in (1, 2, 3):
            z_step(s, d, z).wait_send()
            for h in (0, 1):
                two_step(s, h, d).wait_send()
                spread_step(s, h, 0, d).wait_send()
                spread_step(s, h, 1, d).wait_send()
    for copy in (store_b, store_c, store_d, store_e, store_f, store_g, store_h, store_i):
        copy.wait()


CHUNK = 8


def deliver(out_m, grad_m, sums_m, out_h, grad_h, self_h, nbr_h, bias_h, wout_h, tiles, sums, wide, bias, get, put):
    fetch_sums = pltpu.make_async_copy(sums_m, sums, get.at[16])
    fetch_sums.start()
    moves = []
    for a, (src, dst) in enumerate(((out_m, out_h), (grad_m, grad_h))):
        for s in (0, 1):
            for c in range(NT // CHUNK):
                n = (a * 2 + s) * (NT // CHUNK) + c
                here = tiles.at[n]
                rows = pl.ds(c * CHUNK, CHUNK)
                moves.append(
                    (
                        pltpu.make_async_copy(src.at[s, rows], here, get.at[n]),
                        pltpu.make_async_copy(here, dst.at[s, rows], put.at[n]),
                    )
                )
    for fetch, _ in moves:
        fetch.start()
    fetch_sums.wait()
    wide[...] = sums[:, 0 : 3 * HID].astype(F32)
    for s in (0, 1):
        bias[s : s + 1, :] = sums[s, 3 * HID : 3 * HID + 1].astype(F32)
    rest = [pltpu.make_async_copy(bias, bias_h, put.at[16])]
    for n, dst in enumerate((self_h, nbr_h, wout_h)):
        rest.append(pltpu.make_async_copy(wide.at[:, pl.ds(n * HID, HID)], dst, put.at[17 + n]))
    for copy in rest:
        copy.start()
    for fetch, store in moves:
        fetch.wait()
        store.start()
    for _, store in moves:
        store.wait()
    for copy in rest:
        copy.wait()


def per_device(
    node_in, out_cot, adjacency, tile_nbrs, bound_tiles, live_tiles, w_self, w_nbr, pre_bias, w_out
):
    anyspace = pl.BlockSpec(memory_space=pl.ANY)
    vmem = pl.BlockSpec(memory_space=pltpu.VMEM)
    smem = pl.BlockSpec(memory_space=pltpu.SMEM)
    tiles = lambda n, dtype=BF: pltpu.VMEM((n, ROWS, HID), dtype)
    dma = pltpu.SemaphoreType.DMA
    scratch = [
        pltpu.VMEM((NT, 4, ROWS, ROWS), BF),
        pltpu.VMEM((NT * 4, ROWS, ROWS), BF),
        tiles(NT),
        tiles(LENT),
        tiles(48),
        tiles(48),
        tiles(NT),
        tiles(NT),
        tiles(NT),
        tiles(NT),
        tiles(NT, F32),
        tiles(NT),
        tiles(NT),
        tiles(PAIRS, F32),
        tiles(LENT, F32),
        tiles(NT),
        tiles(LENT),
        tiles(LENT),
        tiles(LENT),
        tiles(LENT),
        pltpu.VMEM((2, 2 * HID, HID), BF),
        pltpu.VMEM((2, HID, HID), BF),
        pltpu.VMEM((2, HID, HID), BF),
        pltpu.VMEM((2, HID, HID), BF),
        pltpu.VMEM((2, HID, HID), BF),
        pltpu.VMEM((2, GRADS, HID), F32),
        pltpu.VMEM((2, GRADS, HID), BF),
        pltpu.VMEM((2, 512, HID), BF),
        pltpu.VMEM((2, 2, 3, 128, 128), BF),
        pltpu.VMEM((2, 2, 3, 32, 128), BF),
        pltpu.VMEM((2, 4, 2, 32, 128), BF),
        pltpu.VMEM((2, GRADS, HID), BF),
        pltpu.VMEM((8, 128), jnp.int32),
        pltpu.SMEM((8, 128), jnp.int32),
        dma((9,)),
        dma,
        dma((8,)),
        dma((4, 2, 8)),
        dma((4, 2, 8)),
        dma((2, 2, 7, 3)),
        dma((2, 2, 7, 3)),
    ]
    out, grad, sums = pl.pallas_call(
        mega,
        out_shape=(
            jax.ShapeDtypeStruct((2, NT, ROWS, HID), BF),
            jax.ShapeDtypeStruct((2, NT, ROWS, HID), BF),
            jax.ShapeDtypeStruct((2, GRADS, HID), BF),
        ),
        in_specs=[
            anyspace, anyspace, anyspace, vmem, smem, smem, smem, anyspace, anyspace, vmem, anyspace,
        ],
        out_specs=(anyspace, anyspace, anyspace),
        scratch_shapes=scratch,
        compiler_params=pltpu.CompilerParams(
            collective_id=0, has_side_effects=True, vmem_limit_bytes=67043328
        ),
        name="mesh_layers",
    )(
        node_in.reshape(NT, ROWS, HID), out_cot.reshape(NT, ROWS, HID), adjacency,
        tile_nbrs.T, tile_nbrs.T, bound_tiles, live_tiles, w_self, w_nbr, pre_bias, w_out,
    )
    square = jax.ShapeDtypeStruct((2, HID, HID), F32)
    out, grad, grad_self, grad_nbr, grad_bias, grad_out = pl.pallas_call(
        deliver,
        out_shape=(
            jax.ShapeDtypeStruct((2, NT, ROWS, HID), BF),
            jax.ShapeDtypeStruct((2, NT, ROWS, HID), BF),
            square,
            square,
            jax.ShapeDtypeStruct((2, HID), F32),
            square,
        ),
        in_specs=[anyspace] * 3,
        out_specs=(anyspace,) * 6,
        scratch_shapes=[
            pltpu.VMEM((16, CHUNK, ROWS, HID), BF),
            pltpu.VMEM((2, GRADS, HID), BF),
            pltpu.VMEM((2, 3 * HID, HID), F32),
            pltpu.VMEM((2, HID), F32),
            dma((17,)),
            dma((20,)),
        ],
        name="deliver",
    )(out, grad, sums)
    rows = NT * ROWS
    return (
        out.reshape(2, rows, HID),
        grad.reshape(2, rows, HID),
        grad_self,
        grad_nbr,
        grad_bias,
        grad_out,
    )


def solution(mesh):
    split = P(AXES)
    in_specs = (split,) * 6 + (P(),) * 4
    out_specs = (P(None, AXES), P(None, AXES), P(), P(), P(), P())
    return jax.shard_map(
        per_device, mesh=mesh, in_specs=in_specs, out_specs=out_specs, check_vma=False
    )
```

```python
import functools

import jax
import jax.numpy as jnp
from jax import lax
from jax.experimental import pallas as pl
from jax.experimental.pallas import tpu as pltpu
from jax.sharding import PartitionSpec as P

AXES = ("dom", "phase", "feat")
MESH = pl.DeviceIdType.MESH
BF = jnp.bfloat16
F32 = jnp.float32
NT = 32
LENT = 16
ROWS = 128
HID = 256
PAIRS = 96
GROUP = 48
GRADS = 1024
UNROLL = 16
AHEAD = 2


def dot(a, b):
    return lax.dot_general(a, b, (((1,), (0,)), ((), ())), preferred_element_type=F32)


def dot_rows(a, b):
    return lax.dot_general(a, b, (((0,), (0,)), ((), ())), preferred_element_type=F32)


def chip_id(x, y, core, z):
    return (x * 4 + (y // 2) * 2 + core, y % 2, z)


def part_id(part):
    return (part // 8, (part // 4) % 2, part % 4)


def build_tables(nbr_vec, bound_sm, tab_v):
    i32 = jnp.int32
    lane32 = lax.broadcasted_iota(i32, (NT, 128), 1)
    row32 = lax.broadcasted_iota(i32, (NT, 128), 0)
    square = lax.broadcasted_iota(i32, (NT, NT), 0) == lax.broadcasted_iota(i32, (NT, NT), 1)
    spread = jnp.zeros((NT, 128), i32)
    for k in range(4):
        line = jnp.broadcast_to(nbr_vec[k : k + 1, :], (NT, NT))
        column = jnp.sum(jnp.where(square, line, 0), axis=1, keepdims=True)
        here = (lane32 // 4 == row32) & (lane32 % 4 == k)
        spread = spread + jnp.where(here, jnp.broadcast_to(column, (NT, 128)), 0)
    target = jnp.sum(spread, axis=0, keepdims=True)
    lane = lax.broadcasted_iota(i32, (1, 128), 1)
    key = jnp.where(lane % 4 == 0, 4096, jnp.where(lane // 4 < LENT, 256, 0) + target)
    li = lax.broadcasted_iota(i32, (128, 128), 1)
    ri = lax.broadcasted_iota(i32, (128, 128), 0)
    key_l = jnp.broadcast_to(key, (128, 128))
    key_c = jnp.sum(jnp.where(li == ri, key_l, 0), axis=1, keepdims=True)
    key_r = jnp.broadcast_to(key_c, (128, 128))
    before = (key_l < key_r) | ((key_l == key_r) & (li < ri))
    rank = jnp.sum(jnp.where(before, 1, 0), axis=1, keepdims=True)
    same = jnp.sum(jnp.where((key_l == key_r) & (li < ri), 1, 0), axis=1, keepdims=True)
    place = jnp.broadcast_to(rank, (128, 128)) == li
    order = jnp.sum(jnp.where(place, ri, 0), axis=0, keepdims=True)
    joins = jnp.sum(jnp.where(place, jnp.broadcast_to(same, (128, 128)), 0), axis=0, keepdims=True)
    slot = lane
    for q in range(LENT):
        slot = jnp.where(lane == bound_sm[0, q // 8, q % 8], q, slot)
    rows = [slot, order, joins]
    for base in (0, 256):
        upto = jnp.sum(jnp.where(key_r <= li + base, 1, 0), axis=0, keepdims=True) - 1
        rows.append(jnp.maximum(upto, 0))
        rows.append(jnp.sum(jnp.where(key_r == li + base, 1, 0), axis=0, keepdims=True))
    for n, row in enumerate(rows):
        tab_v[n : n + 1, :] = row


def mega(
    node_h, cot_h, adj_h, nbr_v, nbr_s, bound_s, live_s, wself_h, wnbr_h, bias_v, wout_h,
    out_h, grad_h, sums_h,
    adj, adj_t, cot, lent, ext0, ext1, agg0, agg1, act0, act1, slope0, dpre, dagg, scan, direct, mid,
    ret1, ret0, send1, send0, w_in, w_out, w_out_t, w_self_t, w_nbr_t,
    total, pack, rc, rx, ry, rz, full, tab_v, tab,
    load_sem, tab_sem, store_sem, hs, hr, gs, gr,
):
    dom, phase, feat = (lax.axis_index(a) for a in AXES)
    x, core = dom // 4, dom % 2
    y = ((dom // 2) % 2) * 2 + phase
    z = feat
    part = dom * 8 + phase * 4 + feat
    west = part_id((part + 127) % 128)
    east = part_id((part + 1) % 128)
    sides = (west, east)
    sibling = chip_id(x, y, 1 - core, z)
    x_ids = [chip_id((x + d) % 4, y, core, z) for d in (1, 2, 3)]
    y_ids = [chip_id(x, (y + d) % 4, core, z) for d in (1, 2, 3)]
    z_ids = [chip_id(x, y, core, (z + d) % 4) for d in (1, 2, 3)]

    loads = [
        pltpu.make_async_copy(node_h.at[pl.ds(0, LENT)], lent, load_sem.at[0]),
        pltpu.make_async_copy(node_h.at[pl.ds(LENT, LENT)], ext0.at[pl.ds(LENT, LENT)], load_sem.at[1]),
        pltpu.make_async_copy(adj_h, adj, load_sem.at[2]),
        pltpu.make_async_copy(wself_h.at[0], w_in.at[0, pl.ds(0, HID)], load_sem.at[3]),
        pltpu.make_async_copy(wself_h.at[1], w_in.at[1, pl.ds(0, HID)], load_sem.at[4]),
        pltpu.make_async_copy(wnbr_h.at[0], w_in.at[0, pl.ds(HID, HID)], load_sem.at[5]),
        pltpu.make_async_copy(wnbr_h.at[1], w_in.at[1, pl.ds(HID, HID)], load_sem.at[6]),
        pltpu.make_async_copy(wout_h, w_out, load_sem.at[7]),
        pltpu.make_async_copy(cot_h, cot, load_sem.at[8]),
    ]
    for copy in loads:
        copy.start()

    barrier = pltpu.get_barrier_semaphore()
    greeted = [west, east, sibling, *x_ids, *y_ids, *z_ids]
    for device in greeted:
        pl.semaphore_signal(barrier, inc=1, device_id=device, device_id_type=MESH)
    pl.semaphore_wait(barrier, len(greeted))

    def remote(src, dst, ssem, rsem, device):
        return pltpu.make_async_remote_copy(
            src_ref=src, dst_ref=dst, send_sem=ssem, recv_sem=rsem, device_id=device, device_id_type=MESH
        )

    def halo(n, src, dst, side, j):
        place = 40 + j if side == 0 else 32 + j
        return remote(src.at[side * 8 + j], dst.at[place], hs.at[n, side, j], hr.at[n, side, j], sides[side])

    def back(n, src, dst, side, j):
        place = 8 + j if side == 0 else j
        return remote(src.at[side * 8 + j], dst.at[place], hs.at[n, side, j], hr.at[n, side, j], sides[side])

    loads[0].wait()

    def give(j, c):
        for side in (0, 1):
            ext0[side * 8 + j] = lent[bound_s[0, side, j]]
            halo(0, ext0, ext0, side, j).start()
        return c

    lax.fori_loop(0, 8, give, 0)

    build_tables(nbr_v[...], bound_s, tab_v)
    tab_copy = pltpu.make_async_copy(tab_v, tab, tab_sem)
    tab_copy.start()
    for copy in loads[1:]:
        copy.wait()
    for s in (0, 1):
        w_out_t[s] = w_out[s].T
        w_self_t[s] = w_in[s, 0:HID].T
        w_nbr_t[s] = w_in[s, HID : 2 * HID].T
        total[s] = jnp.zeros((GRADS, HID), F32)

    tab_copy.wait()
    live = live_s[0]

    def alive(q):
        return jnp.where(q < live, 1.0, 0.0).astype(F32)

    def cot_of(t, masked):
        c = cot[t]
        return (c.astype(F32) * alive(t)).astype(BF) if masked else c

    def tiles_of(group, i, count):
        if group:
            return [(LENT + i * count + n, LENT + i * count + n) for n in range(count)]
        half = count // 2
        return [
            (bound_s[0, side, i * half + n], side * 8 + i * half + n) for n in range(half) for side in (0, 1)
        ]

    def stacked(ref, tiles):
        return jnp.concatenate([ref[q] for _, q in tiles], axis=0)

    def put(ref, tiles, value):
        for n, (_, q) in enumerate(tiles):
            ref[q] = value[n * ROWS : (n + 1) * ROWS]

    def slope_up(group, i, c):
        tiles = tiles_of(group, i, 4)
        m = jnp.concatenate([cot_of(t, group) for t, _ in tiles], axis=0)
        put(scan, tiles, dot(m, w_out_t[1]))
        return c

    def gathered(ext, tiles):
        parts = []
        for t, _ in tiles:
            left = jnp.concatenate([adj[t, k] for k in range(4)], axis=1)
            right = jnp.concatenate([ext[tab[0, nbr_s[k, t]]] for k in range(4)], axis=0)
            parts.append(dot(left, right).astype(BF))
        return jnp.concatenate(parts, axis=0)

    def layer(s, ext, agg, act, tiles):
        f = stacked(ext, tiles)
        a = gathered(ext, tiles)
        put(agg, tiles, a)
        pre = dot(jnp.concatenate([f, a], axis=1), w_in[s]) + bias_v[s : s + 1, :]
        gate = 0.5 * jnp.tanh(0.5 * pre) + 0.5
        hidden = pre * gate
        h = hidden.astype(BF)
        put(act, tiles, h)
        return f, h, gate + hidden * (1.0 - gate)

    def masked_rows(group, tiles, value):
        if not group:
            return value
        return jnp.concatenate(
            [value[n * ROWS : (n + 1) * ROWS] * alive(t) for n, (t, _) in enumerate(tiles)], axis=0
        )

    def first(group, i, c):
        tiles = tiles_of(group, i, 2)
        f, h, slope = layer(0, ext0, agg0, act0, tiles)
        put(slope0, tiles, slope)
        out = masked_rows(group, tiles, f.astype(F32) + dot(h, w_out[0])).astype(BF)
        put(ext1, tiles, out)
        if not group:
            for side in (0, 1):
                halo(1, ext1, ext1, side, i).start()
        return c

    def land(n, ext, j, c):
        for side in (0, 1):
            halo(n, ext, ext, side, j).wait_recv()
        return c

    lax.fori_loop(0, 8, functools.partial(land, 0, ext0), 0)
    lax.fori_loop(0, 8, functools.partial(first, 0), 0)
    lax.fori_loop(0, 8, functools.partial(first, 1), 0)
    lax.fori_loop(0, 4, functools.partial(slope_up, 0), 0)
    lax.fori_loop(0, 4, functools.partial(slope_up, 1), 0)

    def flip(t, c):
        for k in range(4):
            adj_t[t * 4 + k] = adj[t, k].T
        return c

    lax.fori_loop(0, NT, flip, 0)

    lax.fori_loop(0, 8, functools.partial(land, 1, ext1), 0)

    def second(group, i, c):
        tiles = tiles_of(group, i, 4)
        _, _, slope = layer(1, ext1, agg1, act1, tiles)
        d = (stacked(scan, tiles) * slope).astype(BF)
        put(dpre, tiles, d)
        put(dagg, tiles, dot(d, w_nbr_t[1]).astype(BF))
        return c

    lax.fori_loop(0, 4, functools.partial(second, 0), 0, unroll=2)
    lax.fori_loop(0, 4, functools.partial(second, 1), 0, unroll=2)

    def pair(base, i, c):
        begin = base + i * UNROLL
        total_so_far = scan[jnp.maximum(begin - 1, 0)]
        for n in range(UNROLL):
            p = tab[1, begin + n]
            value = dot(adj_t[p], dagg[tab[0, p // 4]])
            keep = tab[2, begin + n] > 0
            total_so_far = value + jnp.where(keep, total_so_far, jnp.zeros_like(value))
            scan[begin + n] = total_so_far
        return c

    def pairs(begin, end):
        lax.fori_loop(0, (end - begin) // UNROLL, functools.partial(pair, begin), 0)

    def collected(target):
        low = scan[tab[3, target]]
        high = scan[tab[5, target]]
        nil = jnp.zeros_like(low)
        return jnp.where(tab[4, target] > 0, low, nil) + jnp.where(tab[6, target] > 0, high, nil)

    def give_back(n, src, dst, j, c):
        for side in (0, 1):
            src[side * 8 + j] = collected(32 + side * 8 + j).astype(BF)
            back(n, src, dst, side, j).start()
        return c

    pairs(0, GROUP)
    pairs(GROUP, PAIRS)
    lax.fori_loop(0, 8, functools.partial(give_back, 2, send1, ret1), 0)

    def unlent(src, dst, t, c):
        dst[t] = src[tab[0, t]]
        return c

    lax.fori_loop(0, LENT, functools.partial(unlent, ext1, send0), 0)
    store_a = pltpu.make_async_copy(send0, out_h.at[0, pl.ds(0, LENT)], store_sem.at[0])
    store_b = pltpu.make_async_copy(ext1.at[pl.ds(LENT, LENT)], out_h.at[0, pl.ds(LENT, LENT)], store_sem.at[1])
    store_a.start()
    store_b.start()

    def straight(s, tiles, m):
        d = dot(stacked(dpre, tiles), w_self_t[s])
        parts = []
        for n, (t, q) in enumerate(tiles):
            own = dot(adj_t[t * 4], dagg[q]) + collected(t)
            parts.append(m[n * ROWS : (n + 1) * ROWS].astype(F32) + d[n * ROWS : (n + 1) * ROWS] + own)
        return jnp.concatenate(parts, axis=0)

    def add_grads(s, ext, agg, act, tiles, m):
        d = stacked(dpre, tiles)
        total[s, 0:HID] += dot_rows(stacked(ext, tiles), d)
        total[s, HID : 2 * HID] += dot_rows(stacked(agg, tiles), d)
        total[s, 2 * HID : 3 * HID] += dot_rows(stacked(act, tiles), m)
        total[s, 3 * HID : 3 * HID + 1] += jnp.sum(d.astype(F32), axis=0, keepdims=True)

    def later_grads(group, i, c):
        tiles = tiles_of(group, i, 4)
        m = jnp.concatenate([cot_of(t, group) for t, _ in tiles], axis=0)
        add_grads(1, ext1, agg1, act1, tiles, m)
        return c

    def later(group, i, c):
        tiles = tiles_of(group, i, 4)
        m = jnp.concatenate([cot_of(t, group) for t, _ in tiles], axis=0)
        value = straight(1, tiles, m)
        if group:
            put(mid, tiles, value.astype(BF))
        else:
            put(direct, tiles, value)
        return c

    def core_step(s):
        return remote(pack.at[s, :, pl.ds((1 - core) * 512, 512)], rc.at[s], gs.at[s, 0, 0, 0], gr.at[s, 0, 0, 0], sibling)

    def order_of(h):
        return ((x, x_ids), (y, y_ids)) if h == 0 else ((y, y_ids), (x, x_ids))

    def columns(h):
        return pl.ds(h * 128, 128)

    def one_step(s, h, d):
        (p, ids), _ = order_of(h)
        rows = pl.ds(core * 512 + ((p + d) % 4) * 128, 128)
        src = pack.at[s, h, rows]
        return remote(src, rx.at[s, h, d - 1], gs.at[s, h, 1, d - 1], gr.at[s, h, 1, d - 1], ids[d - 1])

    def two_step(s, h, d):
        (p, _), (q, ids) = order_of(h)
        rows = pl.ds(core * 512 + p * 128 + ((q + d) % 4) * 32, 32)
        src = pack.at[s, h, rows]
        return remote(src, ry.at[s, h, d - 1], gs.at[s, h, 2, d - 1], gr.at[s, h, 2, d - 1], ids[d - 1])

    def z_step(s, d, slot):
        here = rz.at[s, slot]
        return remote(here, here, gs.at[s, 0, 3, d - 1], gr.at[s, 0, 3, d - 1], z_ids[d - 1])

    def spread_step(s, h, level, d, back_by=0):
        (p, ids_p), (q, ids_q) = order_of(h)
        if level == 0:
            base, size, ids = core * 512 + p * 128 + ((q + 4 - back_by) % 4) * 32, 32, ids_q
        else:
            base, size, ids = core * 512 + ((p + 4 - back_by) % 4) * 128, 128, ids_p
        rows = full.at[s, h, pl.ds(base, size)]
        return remote(rows, rows, gs.at[s, h, 4 + level, d - 1], gr.at[s, h, 4 + level, d - 1], ids[d - 1])

    def half_step(s, half):
        rows = full.at[s, :, pl.ds(half * 512, 512)]
        return remote(rows, rows, gs.at[s, 0, 6, 0], gr.at[s, 0, 6, 0], sibling)

    def sums_begin(s):
        other = pl.ds((1 - core) * 512, 512)
        for h in (0, 1):
            pack[s, h, other] = total[s, other, columns(h)].astype(BF)
        core_step(s).start()

    def sums_x(s):
        core_step(s).wait_recv()
        own = pl.ds(core * 512, 512)
        for h in (0, 1):
            value = total[s, own, columns(h)] + rc[s, h].astype(F32)
            total[s, own, columns(h)] = value
            pack[s, h, own] = value.astype(BF)
        for d in (1, 2, 3):
            for h in (0, 1):
                one_step(s, h, d).start()

    def sums_y(s):
        for h in (0, 1):
            (p, _), _ = order_of(h)
            for d in (1, 2, 3):
                one_step(s, h, d).wait()
            own, cols = pl.ds(core * 512 + p * 128, 128), columns(h)
            value = total[s, own, cols]
            for d in (1, 2, 3):
                value = value + rx[s, h, d - 1].astype(F32)
            total[s, own, cols] = value
            pack[s, h, own] = value.astype(BF)
            for d in (1, 2, 3):
                two_step(s, h, d).start()

    def sums_z(s):
        for h in (0, 1):
            (p, _), (q, _) = order_of(h)
            for d in (1, 2, 3):
                two_step(s, h, d).wait_recv()
            own = pl.ds(core * 512 + p * 128 + q * 32, 32)
            value = total[s, own, columns(h)]
            for d in (1, 2, 3):
                value = value + ry[s, h, d - 1].astype(F32)
            rz[s, z, h] = value.astype(BF)
        for d in (1, 2, 3):
            z_step(s, d, z).start()

    def sums_back(s):
        for d in (1, 2, 3):
            z_step(s, d, (z + 4 - d) % 4).wait_recv()
        for h in (0, 1):
            (p, _), (q, _) = order_of(h)
            value = rz[s, 0, h].astype(F32)
            for n in (1, 2, 3):
                value = value + rz[s, n, h].astype(F32)
            full[s, h, pl.ds(core * 512 + p * 128 + q * 32, 32)] = value.astype(BF)
            for d in (1, 2, 3):
                spread_step(s, h, 0, d).start()

    def sums_up(s, level):
        for h in (0, 1):
            for d in (1, 2, 3):
                spread_step(s, h, level, d, d).wait_recv()
            if level == 0:
                for d in (1, 2, 3):
                    spread_step(s, h, 1, d).start()
        if level == 1:
            half_step(s, core).start()

    def sums_end(s):
        half_step(s, 1 - core).wait_recv()
        store = pltpu.make_async_copy(full.at[s], sums_h.at[s], store_sem.at[6 + s])
        store.start()
        return store

    lax.fori_loop(0, 4, functools.partial(later_grads, 0), 0)
    lax.fori_loop(0, 4, functools.partial(later_grads, 1), 0)
    sums_begin(1)
    lax.fori_loop(0, 4, functools.partial(later, 0), 0)
    lax.fori_loop(0, 4, functools.partial(later, 1), 0)
    sums_x(1)

    def last_out(i, c):
        ts = [i * 4 + n for n in range(4)]
        qs = [tab[0, t] for t in ts]
        h = jnp.concatenate([act1[q] for q in qs], axis=0)
        f = jnp.concatenate([ext1[q] for q in qs], axis=0)
        value = f.astype(F32) + dot(h, w_out[1])
        for n, t in enumerate(ts):
            cot[t] = (value[n * ROWS : (n + 1) * ROWS] * alive(t)).astype(BF)
        return c

    def pull(tiles, m):
        d = (dot(m, w_out_t[0]) * stacked(slope0, tiles)).astype(BF)
        put(dpre, tiles, d)
        put(dagg, tiles, dot(d, w_nbr_t[0]).astype(BF))

    def early_rest(i, c):
        tiles = tiles_of(1, i, 4)
        m = jnp.concatenate([(mid[q].astype(F32) * alive(t)).astype(BF) for t, q in tiles], axis=0)
        pull(tiles, m)
        add_grads(0, ext0, agg0, act0, tiles, m)
        return c

    lax.fori_loop(0, 4, early_rest, 0)
    pairs(0, GROUP)
    lax.fori_loop(0, 8, last_out, 0)
    store_c = pltpu.make_async_copy(cot, out_h.at[1], store_sem.at[2])
    store_c.start()
    store_d = pltpu.make_async_copy(mid.at[pl.ds(LENT, LENT)], grad_h.at[1, pl.ds(LENT, LENT)], store_sem.at[3])
    store_d.start()

    def early(i, c):
        for side in (0, 1):
            back(2, send1, ret1, side, i).wait_recv()
        tiles = tiles_of(0, i, 2)
        m = (stacked(direct, tiles) + stacked(ret1, tiles).astype(F32)).astype(BF)
        put(mid, tiles, m)
        pull(tiles, m)
        add_grads(0, ext0, agg0, act0, tiles, m)
        return c

    lax.fori_loop(0, 8, early, 0)
    sums_begin(0)
    sums_y(1)
    store_a.wait()
    pairs(GROUP, PAIRS)

    def hold_back(j, c):
        for side in (0, 1):
            send0[side * 8 + j] = collected(32 + side * 8 + j).astype(BF)
        return c

    def in_turn(j, c):
        for side in (0, 1):
            back(3, send0, ret0, side, j - AHEAD).wait_send()
            back(3, send0, ret0, side, j).start()
        return c

    lax.fori_loop(0, AHEAD, functools.partial(give_back, 3, send0, ret0), 0)
    sums_x(0)
    lax.fori_loop(AHEAD, 8, hold_back, 0)

    lax.fori_loop(0, LENT, functools.partial(unlent, mid, lent), 0)
    store_e = pltpu.make_async_copy(lent, grad_h.at[1, pl.ds(0, LENT)], store_sem.at[4])
    store_e.start()

    def whole(group, i, c):
        tiles = tiles_of(group, i, 4)
        if group:
            m = jnp.concatenate([(mid[q].astype(F32) * alive(t)).astype(BF) for t, q in tiles], axis=0)
            put(act1, tiles, straight(0, tiles, m).astype(BF))
        else:
            put(direct, tiles, straight(0, tiles, stacked(mid, tiles)))
        return c

    lax.fori_loop(0, 2, functools.partial(whole, 1), 0)
    lax.fori_loop(AHEAD, 4, in_turn, 0)
    sums_y(0)
    lax.fori_loop(4, 6, in_turn, 0)
    lax.fori_loop(2, 4, functools.partial(whole, 1), 0)
    store_f = pltpu.make_async_copy(act1.at[pl.ds(LENT, LENT)], grad_h.at[0, pl.ds(LENT, LENT)], store_sem.at[5])
    store_f.start()
    sums_z(1)
    sums_z(0)
    lax.fori_loop(6, 8, in_turn, 0)
    lax.fori_loop(0, 4, functools.partial(whole, 0), 0)
    sums_back(1)
    sums_back(0)
    sums_up(1, 0)
    sums_up(0, 0)

    def arrive(j, c):
        for side in (0, 1):
            back(3, send0, ret0, side, j).wait_recv()
        return c

    lax.fori_loop(0, 8, arrive, 0)

    def finish(t, c):
        q = tab[0, t]
        act1[t] = (direct[q] + ret0[q].astype(F32)).astype(BF)
        return c

    lax.fori_loop(0, LENT, finish, 0)
    store_g = pltpu.make_async_copy(act1.at[pl.ds(0, LENT)], grad_h.at[0, pl.ds(0, LENT)], store_sem.at[0])
    store_g.start()
    sums_up(1, 1)
    sums_up(0, 1)
    store_h = sums_end(1)
    store_i = sums_end(0)

    def drain(j, c):
        for side in (0, 1):
            halo(0, ext0, ext0, side, j).wait_send()
            halo(1, ext1, ext1, side, j).wait_send()
            back(2, send1, ret1, side, j).wait_send()
        return c

    def drain_last(j, c):
        for side in (0, 1):
            back(3, send0, ret0, side, j).wait_send()
        return c

    lax.fori_loop(0, 8, drain, 0)
    lax.fori_loop(8 - AHEAD, 8, drain_last, 0)
    for s in (1, 0):
        core_step(s).wait_send()
        half_step(s, core).wait_send()
        for d in (1, 2, 3):
            z_step(s, d, z).wait_send()
            for h in (0, 1):
                two_step(s, h, d).wait_send()
                spread_step(s, h, 0, d).wait_send()
                spread_step(s, h, 1, d).wait_send()
    for copy in (store_b, store_c, store_d, store_e, store_f, store_g, store_h, store_i):
        copy.wait()


CHUNK = 8


def deliver(out_m, grad_m, sums_m, out_h, grad_h, self_h, nbr_h, bias_h, wout_h, tiles, sums, wide, bias, get, put):
    fetch_sums = pltpu.make_async_copy(sums_m, sums, get.at[16])
    fetch_sums.start()
    moves = []
    for a, (src, dst) in enumerate(((out_m, out_h), (grad_m, grad_h))):
        for s in (0, 1):
            for c in range(NT // CHUNK):
                n = (a * 2 + s) * (NT // CHUNK) + c
                here = tiles.at[n]
                rows = pl.ds(c * CHUNK, CHUNK)
                moves.append(
                    (
                        pltpu.make_async_copy(src.at[s, rows], here, get.at[n]),
                        pltpu.make_async_copy(here, dst.at[s, rows], put.at[n]),
                    )
                )
    for fetch, _ in moves:
        fetch.start()
    fetch_sums.wait()
    for h in (0, 1):
        cols = pl.ds(h * 128, 128)
        wide[:, :, cols] = sums[:, h, 0 : 3 * HID].astype(F32)
        for s in (0, 1):
            bias[s : s + 1, cols] = sums[s, h, 3 * HID : 3 * HID + 1].astype(F32)
    rest = [pltpu.make_async_copy(bias, bias_h, put.at[16])]
    for n, dst in enumerate((self_h, nbr_h, wout_h)):
        rest.append(pltpu.make_async_copy(wide.at[:, pl.ds(n * HID, HID)], dst, put.at[17 + n]))
    for copy in rest:
        copy.start()
    for fetch, store in moves:
        fetch.wait()
        store.start()
    for _, store in moves:
        store.wait()
    for copy in rest:
        copy.wait()


def per_device(
    node_in, out_cot, adjacency, tile_nbrs, bound_tiles, live_tiles, w_self, w_nbr, pre_bias, w_out
):
    anyspace = pl.BlockSpec(memory_space=pl.ANY)
    vmem = pl.BlockSpec(memory_space=pltpu.VMEM)
    smem = pl.BlockSpec(memory_space=pltpu.SMEM)
    tiles = lambda n, dtype=BF: pltpu.VMEM((n, ROWS, HID), dtype)
    dma = pltpu.SemaphoreType.DMA
    scratch = [
        pltpu.VMEM((NT, 4, ROWS, ROWS), BF),
        pltpu.VMEM((NT * 4, ROWS, ROWS), BF),
        tiles(NT),
        tiles(LENT),
        tiles(48),
        tiles(48),
        tiles(NT),
        tiles(NT),
        tiles(NT),
        tiles(NT),
        tiles(NT, F32),
        tiles(NT),
        tiles(NT),
        tiles(PAIRS, F32),
        tiles(LENT, F32),
        tiles(NT),
        tiles(LENT),
        tiles(LENT),
        tiles(LENT),
        tiles(LENT),
        pltpu.VMEM((2, 2 * HID, HID), BF),
        pltpu.VMEM((2, HID, HID), BF),
        pltpu.VMEM((2, HID, HID), BF),
        pltpu.VMEM((2, HID, HID), BF),
        pltpu.VMEM((2, HID, HID), BF),
        pltpu.VMEM((2, GRADS, HID), F32),
        pltpu.VMEM((2, 2, GRADS, 128), BF),
        pltpu.VMEM((2, 2, 512, 128), BF),
        pltpu.VMEM((2, 2, 3, 128, 128), BF),
        pltpu.VMEM((2, 2, 3, 32, 128), BF),
        pltpu.VMEM((2, 4, 2, 32, 128), BF),
        pltpu.VMEM((2, 2, GRADS, 128), BF),
        pltpu.VMEM((8, 128), jnp.int32),
        pltpu.SMEM((8, 128), jnp.int32),
        dma((9,)),
        dma,
        dma((8,)),
        dma((4, 2, 8)),
        dma((4, 2, 8)),
        dma((2, 2, 7, 3)),
        dma((2, 2, 7, 3)),
    ]
    out, grad, sums = pl.pallas_call(
        mega,
        out_shape=(
            jax.ShapeDtypeStruct((2, NT, ROWS, HID), BF),
            jax.ShapeDtypeStruct((2, NT, ROWS, HID), BF),
            jax.ShapeDtypeStruct((2, 2, GRADS, 128), BF),
        ),
        in_specs=[
            anyspace, anyspace, anyspace, vmem, smem, smem, smem, anyspace, anyspace, vmem, anyspace,
        ],
        out_specs=(anyspace, anyspace, anyspace),
        scratch_shapes=scratch,
        compiler_params=pltpu.CompilerParams(
            collective_id=0, has_side_effects=True, vmem_limit_bytes=67043328
        ),
        name="mesh_layers",
    )(
        node_in.reshape(NT, ROWS, HID), out_cot.reshape(NT, ROWS, HID), adjacency,
        tile_nbrs.T, tile_nbrs.T, bound_tiles, live_tiles, w_self, w_nbr, pre_bias, w_out,
    )
    square = jax.ShapeDtypeStruct((2, HID, HID), F32)
    out, grad, grad_self, grad_nbr, grad_bias, grad_out = pl.pallas_call(
        deliver,
        out_shape=(
            jax.ShapeDtypeStruct((2, NT, ROWS, HID), BF),
            jax.ShapeDtypeStruct((2, NT, ROWS, HID), BF),
            square,
            square,
            jax.ShapeDtypeStruct((2, HID), F32),
            square,
        ),
        in_specs=[anyspace] * 3,
        out_specs=(anyspace,) * 6,
        scratch_shapes=[
            pltpu.VMEM((16, CHUNK, ROWS, HID), BF),
            pltpu.VMEM((2, 2, GRADS, 128), BF),
            pltpu.VMEM((2, 3 * HID, HID), F32),
            pltpu.VMEM((2, HID), F32),
            dma((17,)),
            dma((20,)),
        ],
        name="deliver",
    )(out, grad, sums)
    rows = NT * ROWS
    return (
        out.reshape(2, rows, HID),
        grad.reshape(2, rows, HID),
        grad_self,
        grad_nbr,
        grad_bias,
        grad_out,
    )


def solution(mesh):
    split = P(AXES)
    in_specs = (split,) * 6 + (P(),) * 4
    out_specs = (P(None, AXES), P(None, AXES), P(), P(), P(), P())
    return jax.shard_map(
        per_device, mesh=mesh, in_specs=in_specs, out_specs=out_specs, check_vma=False
    )
```

```python
import functools

import jax
import jax.numpy as jnp
from jax import lax
from jax.experimental import pallas as pl
from jax.experimental.pallas import tpu as pltpu
from jax.sharding import PartitionSpec as P

AXES = ("dom", "phase", "feat")
MESH = pl.DeviceIdType.MESH
BF = jnp.bfloat16
F32 = jnp.float32
NT = 32
LENT = 16
ROWS = 128
HID = 256
PAIRS = 96
GROUP = 48
GRADS = 1024
UNROLL = 48
AHEAD = 2


def dot(a, b):
    return lax.dot_general(a, b, (((1,), (0,)), ((), ())), preferred_element_type=F32)


def dot_rows(a, b):
    return lax.dot_general(a, b, (((0,), (0,)), ((), ())), preferred_element_type=F32)


def chip_id(x, y, core, z):
    return (x * 4 + (y // 2) * 2 + core, y % 2, z)


def part_id(part):
    return (part // 8, (part // 4) % 2, part % 4)


def build_tables(nbr_vec, bound_sm, tab_v):
    i32 = jnp.int32
    lane32 = lax.broadcasted_iota(i32, (NT, 128), 1)
    row32 = lax.broadcasted_iota(i32, (NT, 128), 0)
    square = lax.broadcasted_iota(i32, (NT, NT), 0) == lax.broadcasted_iota(i32, (NT, NT), 1)
    spread = jnp.zeros((NT, 128), i32)
    for k in range(4):
        line = jnp.broadcast_to(nbr_vec[k : k + 1, :], (NT, NT))
        column = jnp.sum(jnp.where(square, line, 0), axis=1, keepdims=True)
        here = (lane32 // 4 == row32) & (lane32 % 4 == k)
        spread = spread + jnp.where(here, jnp.broadcast_to(column, (NT, 128)), 0)
    target = jnp.sum(spread, axis=0, keepdims=True)
    lane = lax.broadcasted_iota(i32, (1, 128), 1)
    key = jnp.where(lane % 4 == 0, 4096, jnp.where(lane // 4 < LENT, 256, 0) + target)
    li = lax.broadcasted_iota(i32, (128, 128), 1)
    ri = lax.broadcasted_iota(i32, (128, 128), 0)
    key_l = jnp.broadcast_to(key, (128, 128))
    key_c = jnp.sum(jnp.where(li == ri, key_l, 0), axis=1, keepdims=True)
    key_r = jnp.broadcast_to(key_c, (128, 128))
    before = (key_l < key_r) | ((key_l == key_r) & (li < ri))
    rank = jnp.sum(jnp.where(before, 1, 0), axis=1, keepdims=True)
    same = jnp.sum(jnp.where((key_l == key_r) & (li < ri), 1, 0), axis=1, keepdims=True)
    place = jnp.broadcast_to(rank, (128, 128)) == li
    order = jnp.sum(jnp.where(place, ri, 0), axis=0, keepdims=True)
    joins = jnp.sum(jnp.where(place, jnp.broadcast_to(same, (128, 128)), 0), axis=0, keepdims=True)
    slot = lane
    for q in range(LENT):
        slot = jnp.where(lane == bound_sm[0, q // 8, q % 8], q, slot)
    rows = [slot, order, joins]
    for base in (0, 256):
        upto = jnp.sum(jnp.where(key_r <= li + base, 1, 0), axis=0, keepdims=True) - 1
        rows.append(jnp.maximum(upto, 0))
        rows.append(jnp.sum(jnp.where(key_r == li + base, 1, 0), axis=0, keepdims=True))
    for n, row in enumerate(rows):
        tab_v[n : n + 1, :] = row


def mega(
    node_h, cot_h, adj_h, nbr_v, nbr_s, bound_s, live_s, wself_h, wnbr_h, bias_v, wout_h,
    out_h, grad_h, sums_h,
    adj, adj_t, cot, lent, ext0, ext1, agg0, agg1, act0, act1, slope0, dpre, dagg, scan, direct, mid,
    ret1, ret0, send1, send0, w_in, w_out, w_out_t, w_self_t, w_nbr_t,
    total, pack, rc, rx, ry, rz, full, tab_v, tab,
    load_sem, tab_sem, store_sem, hs, hr, gs, gr,
):
    dom, phase, feat = (lax.axis_index(a) for a in AXES)
    x, core = dom // 4, dom % 2
    y = ((dom // 2) % 2) * 2 + phase
    z = feat
    part = dom * 8 + phase * 4 + feat
    west = part_id((part + 127) % 128)
    east = part_id((part + 1) % 128)
    sides = (west, east)
    sibling = chip_id(x, y, 1 - core, z)
    x_ids = [chip_id((x + d) % 4, y, core, z) for d in (1, 2, 3)]
    y_ids = [chip_id(x, (y + d) % 4, core, z) for d in (1, 2, 3)]
    z_ids = [chip_id(x, y, core, (z + d) % 4) for d in (1, 2, 3)]

    barrier = pltpu.get_barrier_semaphore()
    greeted = [west, east, sibling, *x_ids, *y_ids, *z_ids]
    for device in greeted:
        pl.semaphore_signal(barrier, inc=1, device_id=device, device_id_type=MESH)

    loads = [
        pltpu.make_async_copy(node_h.at[pl.ds(0, LENT)], lent, load_sem.at[0]),
        pltpu.make_async_copy(node_h.at[pl.ds(LENT, LENT)], ext0.at[pl.ds(LENT, LENT)], load_sem.at[1]),
        pltpu.make_async_copy(adj_h, adj, load_sem.at[2]),
        pltpu.make_async_copy(wself_h.at[0], w_in.at[0, pl.ds(0, HID)], load_sem.at[3]),
        pltpu.make_async_copy(wself_h.at[1], w_in.at[1, pl.ds(0, HID)], load_sem.at[4]),
        pltpu.make_async_copy(wnbr_h.at[0], w_in.at[0, pl.ds(HID, HID)], load_sem.at[5]),
        pltpu.make_async_copy(wnbr_h.at[1], w_in.at[1, pl.ds(HID, HID)], load_sem.at[6]),
        pltpu.make_async_copy(wout_h, w_out, load_sem.at[7]),
        pltpu.make_async_copy(cot_h, cot, load_sem.at[8]),
    ]
    for copy in loads:
        copy.start()

    pl.semaphore_wait(barrier, len(greeted))

    def remote(src, dst, ssem, rsem, device):
        return pltpu.make_async_remote_copy(
            src_ref=src, dst_ref=dst, send_sem=ssem, recv_sem=rsem, device_id=device, device_id_type=MESH
        )

    def halo(n, src, dst, side, j):
        place = 40 + j if side == 0 else 32 + j
        return remote(src.at[side * 8 + j], dst.at[place], hs.at[n, side, j], hr.at[n, side, j], sides[side])

    def back(n, src, dst, side, j):
        place = 8 + j if side == 0 else j
        return remote(src.at[side * 8 + j], dst.at[place], hs.at[n, side, j], hr.at[n, side, j], sides[side])

    loads[0].wait()

    def give(j, c):
        for side in (0, 1):
            ext0[side * 8 + j] = lent[bound_s[0, side, j]]
            halo(0, ext0, ext0, side, j).start()
        return c

    lax.fori_loop(0, 8, give, 0)

    build_tables(nbr_v[...], bound_s, tab_v)
    tab_copy = pltpu.make_async_copy(tab_v, tab, tab_sem)
    tab_copy.start()
    for copy in loads[1:]:
        copy.wait()
    for s in (0, 1):
        w_out_t[s] = w_out[s].T
        w_self_t[s] = w_in[s, 0:HID].T
        w_nbr_t[s] = w_in[s, HID : 2 * HID].T
        total[s] = jnp.zeros((GRADS, HID), F32)

    tab_copy.wait()
    live = live_s[0]

    def alive(q):
        return jnp.where(q < live, 1.0, 0.0).astype(F32)

    def cot_of(t, masked):
        c = cot[t]
        return (c.astype(F32) * alive(t)).astype(BF) if masked else c

    def tiles_of(group, i, count):
        if group:
            return [(LENT + i * count + n, LENT + i * count + n) for n in range(count)]
        half = count // 2
        return [
            (bound_s[0, side, i * half + n], side * 8 + i * half + n) for n in range(half) for side in (0, 1)
        ]

    def stacked(ref, tiles):
        return jnp.concatenate([ref[q] for _, q in tiles], axis=0)

    def put(ref, tiles, value):
        for n, (_, q) in enumerate(tiles):
            ref[q] = value[n * ROWS : (n + 1) * ROWS]

    def slope_up(group, i, c):
        tiles = tiles_of(group, i, 4)
        m = jnp.concatenate([cot_of(t, group) for t, _ in tiles], axis=0)
        put(scan, tiles, dot(m, w_out_t[1]))
        return c

    def gathered(ext, tiles):
        parts = []
        for t, _ in tiles:
            left = jnp.concatenate([adj[t, k] for k in range(4)], axis=1)
            right = jnp.concatenate([ext[tab[0, nbr_s[k, t]]] for k in range(4)], axis=0)
            parts.append(dot(left, right).astype(BF))
        return jnp.concatenate(parts, axis=0)

    def layer(s, ext, agg, act, tiles):
        f = stacked(ext, tiles)
        a = gathered(ext, tiles)
        put(agg, tiles, a)
        pre = dot(jnp.concatenate([f, a], axis=1), w_in[s]) + bias_v[s : s + 1, :]
        gate = 0.5 * jnp.tanh(0.5 * pre) + 0.5
        hidden = pre * gate
        h = hidden.astype(BF)
        put(act, tiles, h)
        return f, h, gate + hidden * (1.0 - gate)

    def masked_rows(group, tiles, value):
        if not group:
            return value
        return jnp.concatenate(
            [value[n * ROWS : (n + 1) * ROWS] * alive(t) for n, (t, _) in enumerate(tiles)], axis=0
        )

    def first(group, i, c):
        tiles = tiles_of(group, i, 2)
        f, h, slope = layer(0, ext0, agg0, act0, tiles)
        put(slope0, tiles, slope)
        out = masked_rows(group, tiles, f.astype(F32) + dot(h, w_out[0])).astype(BF)
        put(ext1, tiles, out)
        if not group:
            for side in (0, 1):
                halo(1, ext1, ext1, side, i).start()
        return c

    def land(n, ext, j, c):
        for side in (0, 1):
            halo(n, ext, ext, side, j).wait_recv()
        return c

    lax.fori_loop(0, 8, functools.partial(land, 0, ext0), 0)
    lax.fori_loop(0, 8, functools.partial(first, 0), 0)
    lax.fori_loop(0, 8, functools.partial(first, 1), 0)
    lax.fori_loop(0, 4, functools.partial(slope_up, 0), 0)
    lax.fori_loop(0, 4, functools.partial(slope_up, 1), 0)

    def flip(t, c):
        for k in range(4):
            adj_t[t * 4 + k] = adj[t, k].T
        return c

    lax.fori_loop(0, NT, flip, 0)

    lax.fori_loop(0, 8, functools.partial(land, 1, ext1), 0)

    def second(group, i, c):
        tiles = tiles_of(group, i, 4)
        _, _, slope = layer(1, ext1, agg1, act1, tiles)
        d = (stacked(scan, tiles) * slope).astype(BF)
        put(dpre, tiles, d)
        put(dagg, tiles, dot(d, w_nbr_t[1]).astype(BF))
        return c

    lax.fori_loop(0, 4, functools.partial(second, 0), 0, unroll=4)
    lax.fori_loop(0, 4, functools.partial(second, 1), 0, unroll=4)

    def pair(base, i, c):
        begin = base + i * UNROLL
        total_so_far = scan[jnp.maximum(begin - 1, 0)]
        for n in range(UNROLL):
            p = tab[1, begin + n]
            value = dot(adj_t[p], dagg[tab[0, p // 4]])
            keep = tab[2, begin + n] > 0
            total_so_far = value + jnp.where(keep, total_so_far, jnp.zeros_like(value))
            scan[begin + n] = total_so_far
        return c

    def pairs(begin, end):
        lax.fori_loop(0, (end - begin) // UNROLL, functools.partial(pair, begin), 0)

    def collected(target):
        low = scan[tab[3, target]]
        high = scan[tab[5, target]]
        nil = jnp.zeros_like(low)
        return jnp.where(tab[4, target] > 0, low, nil) + jnp.where(tab[6, target] > 0, high, nil)

    def give_back(n, src, dst, j, c):
        for side in (0, 1):
            src[side * 8 + j] = collected(32 + side * 8 + j).astype(BF)
            back(n, src, dst, side, j).start()
        return c

    pairs(0, GROUP)
    pairs(GROUP, PAIRS)
    lax.fori_loop(0, 8, functools.partial(give_back, 2, send1, ret1), 0)

    def unlent(src, dst, t, c):
        dst[t] = src[tab[0, t]]
        return c

    lax.fori_loop(0, LENT, functools.partial(unlent, ext1, send0), 0)
    store_a = pltpu.make_async_copy(send0, out_h.at[0, pl.ds(0, LENT)], store_sem.at[0])
    store_b = pltpu.make_async_copy(ext1.at[pl.ds(LENT, LENT)], out_h.at[0, pl.ds(LENT, LENT)], store_sem.at[1])
    store_a.start()
    store_b.start()

    def straight(s, tiles, m):
        d = dot(stacked(dpre, tiles), w_self_t[s])
        parts = []
        for n, (t, q) in enumerate(tiles):
            own = dot(adj_t[t * 4], dagg[q]) + collected(t)
            parts.append(m[n * ROWS : (n + 1) * ROWS].astype(F32) + d[n * ROWS : (n + 1) * ROWS] + own)
        return jnp.concatenate(parts, axis=0)

    def add_grads(s, ext, agg, act, tiles, m):
        d = stacked(dpre, tiles)
        total[s, 0:HID] += dot_rows(stacked(ext, tiles), d)
        total[s, HID : 2 * HID] += dot_rows(stacked(agg, tiles), d)
        total[s, 2 * HID : 3 * HID] += dot_rows(stacked(act, tiles), m)
        total[s, 3 * HID : 3 * HID + 1] += jnp.sum(d.astype(F32), axis=0, keepdims=True)

    def later_grads(group, i, c):
        tiles = tiles_of(group, i, 4)
        m = jnp.concatenate([cot_of(t, group) for t, _ in tiles], axis=0)
        add_grads(1, ext1, agg1, act1, tiles, m)
        return c

    def later(group, i, c):
        tiles = tiles_of(group, i, 4)
        m = jnp.concatenate([cot_of(t, group) for t, _ in tiles], axis=0)
        value = straight(1, tiles, m)
        if group:
            put(mid, tiles, value.astype(BF))
        else:
            put(direct, tiles, value)
        return c

    def core_step(s):
        return remote(pack.at[s, :, pl.ds((1 - core) * 512, 512)], rc.at[s], gs.at[s, 0, 0, 0], gr.at[s, 0, 0, 0], sibling)

    def order_of(h):
        return ((x, x_ids), (y, y_ids)) if h == 0 else ((y, y_ids), (x, x_ids))

    def columns(h):
        return pl.ds(h * 128, 128)

    def one_step(s, h, d):
        (p, ids), _ = order_of(h)
        rows = pl.ds(core * 512 + ((p + d) % 4) * 128, 128)
        src = pack.at[s, h, rows]
        return remote(src, rx.at[s, h, d - 1], gs.at[s, h, 1, d - 1], gr.at[s, h, 1, d - 1], ids[d - 1])

    def two_step(s, h, d):
        (p, _), (q, ids) = order_of(h)
        rows = pl.ds(core * 512 + p * 128 + ((q + d) % 4) * 32, 32)
        src = pack.at[s, h, rows]
        return remote(src, ry.at[s, h, d - 1], gs.at[s, h, 2, d - 1], gr.at[s, h, 2, d - 1], ids[d - 1])

    def z_step(s, d, slot):
        here = rz.at[s, slot]
        return remote(here, here, gs.at[s, 0, 3, d - 1], gr.at[s, 0, 3, d - 1], z_ids[d - 1])

    def spread_step(s, h, level, d, back_by=0):
        (p, ids_p), (q, ids_q) = order_of(h)
        if level == 0:
            base, size, ids = core * 512 + p * 128 + ((q + 4 - back_by) % 4) * 32, 32, ids_q
        else:
            base, size, ids = core * 512 + ((p + 4 - back_by) % 4) * 128, 128, ids_p
        rows = full.at[s, h, pl.ds(base, size)]
        return remote(rows, rows, gs.at[s, h, 4 + level, d - 1], gr.at[s, h, 4 + level, d - 1], ids[d - 1])

    def half_step(s, half):
        rows = full.at[s, :, pl.ds(half * 512, 512)]
        return remote(rows, rows, gs.at[s, 0, 6, 0], gr.at[s, 0, 6, 0], sibling)

    def sums_begin(s):
        other = pl.ds((1 - core) * 512, 512)
        for h in (0, 1):
            pack[s, h, other] = total[s, other, columns(h)].astype(BF)
        core_step(s).start()

    def sums_x(s):
        core_step(s).wait_recv()
        own = pl.ds(core * 512, 512)
        for h in (0, 1):
            value = total[s, own, columns(h)] + rc[s, h].astype(F32)
            total[s, own, columns(h)] = value
            pack[s, h, own] = value.astype(BF)
        for d in (1, 2, 3):
            for h in (0, 1):
                one_step(s, h, d).start()

    def sums_y(s):
        for h in (0, 1):
            (p, _), _ = order_of(h)
            for d in (1, 2, 3):
                one_step(s, h, d).wait()
            own, cols = pl.ds(core * 512 + p * 128, 128), columns(h)
            value = total[s, own, cols]
            for d in (1, 2, 3):
                value = value + rx[s, h, d - 1].astype(F32)
            total[s, own, cols] = value
            pack[s, h, own] = value.astype(BF)
            for d in (1, 2, 3):
                two_step(s, h, d).start()

    def sums_z(s):
        for h in (0, 1):
            (p, _), (q, _) = order_of(h)
            for d in (1, 2, 3):
                two_step(s, h, d).wait_recv()
            own = pl.ds(core * 512 + p * 128 + q * 32, 32)
            value = total[s, own, columns(h)]
            for d in (1, 2, 3):
                value = value + ry[s, h, d - 1].astype(F32)
            rz[s, z, h] = value.astype(BF)
        for d in (1, 2, 3):
            z_step(s, d, z).start()

    def sums_back(s):
        for d in (1, 2, 3):
            z_step(s, d, (z + 4 - d) % 4).wait_recv()
        for h in (0, 1):
            (p, _), (q, _) = order_of(h)
            value = rz[s, 0, h].astype(F32)
            for n in (1, 2, 3):
                value = value + rz[s, n, h].astype(F32)
            full[s, h, pl.ds(core * 512 + p * 128 + q * 32, 32)] = value.astype(BF)
            for d in (1, 2, 3):
                spread_step(s, h, 0, d).start()

    def sums_up(s, level):
        for h in (0, 1):
            for d in (1, 2, 3):
                spread_step(s, h, level, d, d).wait_recv()
            if level == 0:
                for d in (1, 2, 3):
                    spread_step(s, h, 1, d).start()
        if level == 1:
            half_step(s, core).start()

    def sums_end(s):
        half_step(s, 1 - core).wait_recv()
        store = pltpu.make_async_copy(full.at[s], sums_h.at[s], store_sem.at[6 + s])
        store.start()
        return store

    lax.fori_loop(0, 4, functools.partial(later_grads, 0), 0)
    lax.fori_loop(0, 4, functools.partial(later_grads, 1), 0)
    sums_begin(1)
    lax.fori_loop(0, 4, functools.partial(later, 0), 0)
    lax.fori_loop(0, 4, functools.partial(later, 1), 0)
    sums_x(1)

    def last_out(i, c):
        ts = [i * 4 + n for n in range(4)]
        qs = [tab[0, t] for t in ts]
        h = jnp.concatenate([act1[q] for q in qs], axis=0)
        f = jnp.concatenate([ext1[q] for q in qs], axis=0)
        value = f.astype(F32) + dot(h, w_out[1])
        for n, t in enumerate(ts):
            cot[t] = (value[n * ROWS : (n + 1) * ROWS] * alive(t)).astype(BF)
        return c

    def pull(tiles, m):
        d = (dot(m, w_out_t[0]) * stacked(slope0, tiles)).astype(BF)
        put(dpre, tiles, d)
        put(dagg, tiles, dot(d, w_nbr_t[0]).astype(BF))

    def early_rest(i, c):
        tiles = tiles_of(1, i, 4)
        m = jnp.concatenate([(mid[q].astype(F32) * alive(t)).astype(BF) for t, q in tiles], axis=0)
        pull(tiles, m)
        add_grads(0, ext0, agg0, act0, tiles, m)
        return c

    lax.fori_loop(0, 4, early_rest, 0)
    pairs(0, GROUP)
    lax.fori_loop(0, 8, last_out, 0)
    store_c = pltpu.make_async_copy(cot, out_h.at[1], store_sem.at[2])
    store_c.start()
    store_d = pltpu.make_async_copy(mid.at[pl.ds(LENT, LENT)], grad_h.at[1, pl.ds(LENT, LENT)], store_sem.at[3])
    store_d.start()

    def early(i, c):
        for side in (0, 1):
            back(2, send1, ret1, side, i).wait_recv()
        tiles = tiles_of(0, i, 2)
        m = (stacked(direct, tiles) + stacked(ret1, tiles).astype(F32)).astype(BF)
        put(mid, tiles, m)
        pull(tiles, m)
        add_grads(0, ext0, agg0, act0, tiles, m)
        return c

    lax.fori_loop(0, 8, early, 0)
    sums_begin(0)
    sums_y(1)
    store_a.wait()
    pairs(GROUP, PAIRS)

    def hold_back(j, c):
        for side in (0, 1):
            send0[side * 8 + j] = collected(32 + side * 8 + j).astype(BF)
        return c

    def in_turn(j, c):
        for side in (0, 1):
            back(3, send0, ret0, side, j - AHEAD).wait_send()
            back(3, send0, ret0, side, j).start()
        return c

    lax.fori_loop(0, AHEAD, functools.partial(give_back, 3, send0, ret0), 0)
    sums_x(0)
    lax.fori_loop(AHEAD, 8, hold_back, 0)

    lax.fori_loop(0, LENT, functools.partial(unlent, mid, lent), 0)
    store_e = pltpu.make_async_copy(lent, grad_h.at[1, pl.ds(0, LENT)], store_sem.at[4])
    store_e.start()

    def whole(group, i, c):
        tiles = tiles_of(group, i, 4)
        if group:
            m = jnp.concatenate([(mid[q].astype(F32) * alive(t)).astype(BF) for t, q in tiles], axis=0)
            put(act1, tiles, straight(0, tiles, m).astype(BF))
        else:
            put(direct, tiles, straight(0, tiles, stacked(mid, tiles)))
        return c

    lax.fori_loop(0, 2, functools.partial(whole, 1), 0)
    lax.fori_loop(AHEAD, 4, in_turn, 0)
    sums_y(0)
    lax.fori_loop(4, 6, in_turn, 0)
    lax.fori_loop(2, 4, functools.partial(whole, 1), 0)
    store_f = pltpu.make_async_copy(act1.at[pl.ds(LENT, LENT)], grad_h.at[0, pl.ds(LENT, LENT)], store_sem.at[5])
    store_f.start()
    sums_z(1)
    sums_z(0)
    lax.fori_loop(6, 8, in_turn, 0)
    lax.fori_loop(0, 4, functools.partial(whole, 0), 0)
    sums_back(1)
    sums_back(0)
    sums_up(1, 0)
    sums_up(0, 0)

    def arrive(j, c):
        for side in (0, 1):
            back(3, send0, ret0, side, j).wait_recv()
        return c

    lax.fori_loop(0, 8, arrive, 0)

    def finish(t, c):
        q = tab[0, t]
        act1[t] = (direct[q] + ret0[q].astype(F32)).astype(BF)
        return c

    lax.fori_loop(0, LENT, finish, 0)
    store_g = pltpu.make_async_copy(act1.at[pl.ds(0, LENT)], grad_h.at[0, pl.ds(0, LENT)], store_sem.at[0])
    store_g.start()
    sums_up(1, 1)
    sums_up(0, 1)
    store_h = sums_end(1)
    store_i = sums_end(0)

    def drain(j, c):
        for side in (0, 1):
            halo(0, ext0, ext0, side, j).wait_send()
            halo(1, ext1, ext1, side, j).wait_send()
            back(2, send1, ret1, side, j).wait_send()
        return c

    def drain_last(j, c):
        for side in (0, 1):
            back(3, send0, ret0, side, j).wait_send()
        return c

    lax.fori_loop(0, 8, drain, 0)
    lax.fori_loop(8 - AHEAD, 8, drain_last, 0)
    for s in (1, 0):
        core_step(s).wait_send()
        half_step(s, core).wait_send()
        for d in (1, 2, 3):
            z_step(s, d, z).wait_send()
            for h in (0, 1):
                two_step(s, h, d).wait_send()
                spread_step(s, h, 0, d).wait_send()
                spread_step(s, h, 1, d).wait_send()
    for copy in (store_b, store_c, store_d, store_e, store_f, store_g, store_h, store_i):
        copy.wait()


CHUNK = 16
CHUNKS = 4 * NT // CHUNK


def deliver(out_m, grad_m, sums_m, out_h, grad_h, self_h, nbr_h, bias_h, wout_h, tiles, sums, wide, bias, get, put):
    fetch_sums = pltpu.make_async_copy(sums_m, sums, get.at[CHUNKS])
    fetch_sums.start()
    moves = []
    for a, (src, dst) in enumerate(((out_m, out_h), (grad_m, grad_h))):
        for s in (0, 1):
            for c in range(NT // CHUNK):
                n = (a * 2 + s) * (NT // CHUNK) + c
                here = tiles.at[n]
                rows = pl.ds(c * CHUNK, CHUNK)
                moves.append(
                    (
                        pltpu.make_async_copy(src.at[s, rows], here, get.at[n]),
                        pltpu.make_async_copy(here, dst.at[s, rows], put.at[n]),
                    )
                )
    for fetch, _ in moves:
        fetch.start()
    fetch_sums.wait()
    for h in (0, 1):
        cols = pl.ds(h * 128, 128)
        wide[:, :, cols] = sums[:, h, 0 : 3 * HID].astype(F32)
        for s in (0, 1):
            bias[s : s + 1, cols] = sums[s, h, 3 * HID : 3 * HID + 1].astype(F32)
    rest = [pltpu.make_async_copy(bias, bias_h, put.at[CHUNKS])]
    for n, dst in enumerate((self_h, nbr_h, wout_h)):
        rest.append(pltpu.make_async_copy(wide.at[:, pl.ds(n * HID, HID)], dst, put.at[CHUNKS + 1 + n]))
    for copy in rest:
        copy.start()
    for fetch, store in moves:
        fetch.wait()
        store.start()
    for _, store in moves:
        store.wait()
    for copy in rest:
        copy.wait()


def per_device(
    node_in, out_cot, adjacency, tile_nbrs, bound_tiles, live_tiles, w_self, w_nbr, pre_bias, w_out
):
    anyspace = pl.BlockSpec(memory_space=pl.ANY)
    vmem = pl.BlockSpec(memory_space=pltpu.VMEM)
    smem = pl.BlockSpec(memory_space=pltpu.SMEM)
    tiles = lambda n, dtype=BF: pltpu.VMEM((n, ROWS, HID), dtype)
    dma = pltpu.SemaphoreType.DMA
    scratch = [
        pltpu.VMEM((NT, 4, ROWS, ROWS), BF),
        pltpu.VMEM((NT * 4, ROWS, ROWS), BF),
        tiles(NT),
        tiles(LENT),
        tiles(48),
        tiles(48),
        tiles(NT),
        tiles(NT),
        tiles(NT),
        tiles(NT),
        tiles(NT, F32),
        tiles(NT),
        tiles(NT),
        tiles(PAIRS, F32),
        tiles(LENT, F32),
        tiles(NT),
        tiles(LENT),
        tiles(LENT),
        tiles(LENT),
        tiles(LENT),
        pltpu.VMEM((2, 2 * HID, HID), BF),
        pltpu.VMEM((2, HID, HID), BF),
        pltpu.VMEM((2, HID, HID), BF),
        pltpu.VMEM((2, HID, HID), BF),
        pltpu.VMEM((2, HID, HID), BF),
        pltpu.VMEM((2, GRADS, HID), F32),
        pltpu.VMEM((2, 2, GRADS, 128), BF),
        pltpu.VMEM((2, 2, 512, 128), BF),
        pltpu.VMEM((2, 2, 3, 128, 128), BF),
        pltpu.VMEM((2, 2, 3, 32, 128), BF),
        pltpu.VMEM((2, 4, 2, 32, 128), BF),
        pltpu.VMEM((2, 2, GRADS, 128), BF),
        pltpu.VMEM((8, 128), jnp.int32),
        pltpu.SMEM((8, 128), jnp.int32),
        dma((9,)),
        dma,
        dma((8,)),
        dma((4, 2, 8)),
        dma((4, 2, 8)),
        dma((2, 2, 7, 3)),
        dma((2, 2, 7, 3)),
    ]
    out, grad, sums = pl.pallas_call(
        mega,
        out_shape=(
            jax.ShapeDtypeStruct((2, NT, ROWS, HID), BF),
            jax.ShapeDtypeStruct((2, NT, ROWS, HID), BF),
            jax.ShapeDtypeStruct((2, 2, GRADS, 128), BF),
        ),
        in_specs=[
            anyspace, anyspace, anyspace, vmem, smem, smem, smem, anyspace, anyspace, vmem, anyspace,
        ],
        out_specs=(anyspace, anyspace, anyspace),
        scratch_shapes=scratch,
        compiler_params=pltpu.CompilerParams(
            collective_id=0, has_side_effects=True, vmem_limit_bytes=67043328
        ),
        name="mesh_layers",
    )(
        node_in.reshape(NT, ROWS, HID), out_cot.reshape(NT, ROWS, HID), adjacency,
        tile_nbrs.T, tile_nbrs.T, bound_tiles, live_tiles, w_self, w_nbr, pre_bias, w_out,
    )
    square = jax.ShapeDtypeStruct((2, HID, HID), F32)
    out, grad, grad_self, grad_nbr, grad_bias, grad_out = pl.pallas_call(
        deliver,
        out_shape=(
            jax.ShapeDtypeStruct((2, NT, ROWS, HID), BF),
            jax.ShapeDtypeStruct((2, NT, ROWS, HID), BF),
            square,
            square,
            jax.ShapeDtypeStruct((2, HID), F32),
            square,
        ),
        in_specs=[anyspace] * 3,
        out_specs=(anyspace,) * 6,
        scratch_shapes=[
            pltpu.VMEM((CHUNKS, CHUNK, ROWS, HID), BF),
            pltpu.VMEM((2, 2, GRADS, 128), BF),
            pltpu.VMEM((2, 3 * HID, HID), F32),
            pltpu.VMEM((2, HID), F32),
            dma((CHUNKS + 1,)),
            dma((CHUNKS + 4,)),
        ],
        name="deliver",
    )(out, grad, sums)
    rows = NT * ROWS
    return (
        out.reshape(2, rows, HID),
        grad.reshape(2, rows, HID),
        grad_self,
        grad_nbr,
        grad_bias,
        grad_out,
    )


def solution(mesh):
    split = P(AXES)
    in_specs = (split,) * 6 + (P(),) * 4
    out_specs = (P(None, AXES), P(None, AXES), P(), P(), P(), P())
    return jax.shard_map(
        per_device, mesh=mesh, in_specs=in_specs, out_specs=out_specs, check_vma=False
    )
```
